32 devices in a mesh: slab: 4 (over y, x), dom: 8 (over z, core).
Axes of the slice: x: 2, y: 2, z: 4, core: 2. Of those that a mesh axis runs over, the one named last changes fastest.
Arguments:
- tiles: bfloat16 [2560, 128, 128], P('dom'), may hold values from -0.09375 to 0.09375
- volume: float32 [256, 128, 128], P(('slab', 'dom')), parts along dimension 0, may hold values from 0 to 2
- tile_voxel: int32 [2560], P('dom'), may hold values from 0 to 7
- tile_dest: int32 [2560], P('dom'), may hold values from 0 to 7
- slot_block: int32 [8, 8], P('dom'), may hold values from 0 to 7
- tile_count: int32 [8], P('dom'), may hold values from 80 to 320, as said below
- counts: int32 [256, 128, 128], P(('slab', 'dom')), parts along dimension 0, may hold values from 2000 to 29999
Outputs:
- updated: float32 [256, 128, 128], P(('slab', 'dom')), parts along dimension 0
- residual: bfloat16 [256, 128, 128], P(('slab', 'dom')), parts along dimension 0
The draws below stay inside these ranges and needn't reach their ends.
There are 4 independent parts, one for each index of `slab`. The reference program is written for one: setup_inputs(seed, part) draws one part's arguments, and reference() takes and returns one part's arrays. A program takes and returns all parts, laid end to end along the dimension named above; an argument that names none is the same for every part. Nothing has to cross between parts.
Inputs may be any that keep to these rules, and one draw needn't show every extreme that they name: `tile_count`: every device holds at least max(80, 3) live tiles; some device holds 320.
All inputs are finite; a program needn't handle non-finite values.
Results may differ from the reference program's by a relative error of at most 0.006.
Values may be sent and summed in bfloat16 or wider, within the bound.
A program may use at most 128 MiB of HBM per device.

```python
import jax
import jax.numpy as jnp
from jax import lax

TILE = 128
SLICES = 128
TPD = 320
VBD = 8
RBD = 8
VOXBLK = 64
RAYBLK = 64
ALLTILES = 2560
N_DOM = 8


def draw_tile_count(key, part):
    first, second = jax.random.split(jax.random.fold_in(key, 11))
    lowest = max(TPD // 4, 3)
    base = jax.random.randint(first, (N_DOM,), lowest, max(TPD // 2, lowest) + 1)
    busiest = jax.random.randint(second, (), 0, N_DOM)
    return jnp.where(jnp.arange(N_DOM) == busiest, TPD, base).astype(jnp.int32)


def draw_tile_dest(key, part):
    source = jax.random.fold_in(key, 23)
    base = jax.random.randint(source, (N_DOM, TPD), 0, N_DOM)
    holder = jnp.arange(N_DOM, dtype=jnp.int32)
    base = base.at[:, 0].set((holder + 1) % N_DOM)
    base = base.at[:, 1].set((holder + N_DOM // 2) % N_DOM)
    base = base.at[:, 2].set((holder + N_DOM - 1) % N_DOM)
    return base.reshape(N_DOM * TPD).astype(jnp.int32)


def with_ends(result, own_key, smallest, largest):
    shape = result.shape
    index_at = [jax.random.randint(jax.random.fold_in(own_key, axis), (), 0, shape[axis]) for axis in range(len(shape))]
    result = result.at[tuple(index_at)].set(smallest)
    longest = shape.index(max(shape))
    index_at[longest] = (index_at[longest] + 1) % shape[longest]
    return result.at[tuple(index_at)].set(largest)


def steps_of(rng, extent, shards, smallest, top_value):
    gain = 1.0
    for dim, parts in shards:
        steps = jax.random.uniform(jax.random.fold_in(jax.random.fold_in(rng, 6), dim), (parts,), jnp.float32, smallest / len(shards), top_value / len(shards))
        gain = gain * jnp.repeat(jnp.exp(steps), extent[dim] // parts).reshape((-1,) + (1,) * (len(extent) - 1 - dim))
    return gain


def bell_draw(key, shape, width, bound, pieces=(), held_as=jnp.bfloat16):
    array = jax.random.normal(key, shape, jnp.float32) * width
    if len(pieces) > 0:
        array = steps_of(key, shape, pieces, -0.22, 0.18) * array
    return jnp.clip(array, min=-bound, max=bound).astype(held_as)


def setup_inputs(seed: int = 0, part: int = 0) -> dict:
    seeds = jax.random.split(jax.random.key(seed), 8)
    part_splits = jax.random.split(jax.random.fold_in(seeds[7], part), 8)
    tiles = bell_draw(seeds[0], (ALLTILES, TILE, TILE), (TILE * 32) ** -0.5, 0.09375, ((0, 8),))
    volume = jnp.clip(2.0 * jax.random.uniform(part_splits[1], (VOXBLK, TILE, SLICES), jnp.float32) ** steps_of(part_splits[1], (VOXBLK, TILE, SLICES), ((0, 8),), -0.2, 0.2), 0.0, 2.0)
    tile_voxel = with_ends(jax.random.randint(seeds[2], (ALLTILES,), 0, VBD), jax.random.fold_in(seeds[2], 1), 0, VBD - 1).astype(jnp.int32)
    tile_dest = draw_tile_dest(jax.random.fold_in(seeds[7], 71), part)
    slot_block = with_ends(jax.random.randint(seeds[4], (N_DOM, N_DOM), 0, RBD), jax.random.fold_in(seeds[4], 1), 0, RBD - 1).astype(jnp.int32)
    tile_count = draw_tile_count(jax.random.fold_in(seeds[7], 71), part)
    counts = with_ends(jax.random.randint(part_splits[6], (RAYBLK, TILE, SLICES), 2000, 30000), jax.random.fold_in(part_splits[6], 1), 2000, 29999).astype(jnp.int32)
    return dict(tiles=tiles, volume=volume, tile_voxel=tile_voxel, tile_dest=tile_dest, slot_block=slot_block, tile_count=tile_count, counts=counts)


flux = 32768.0
step_size = 0.5


def reference(tiles, volume, tile_voxel, tile_dest, slot_block, tile_count, counts):
    voxels_low = volume.astype(jnp.bfloat16)
    slots = jnp.arange(N_DOM * TPD, dtype=jnp.int32)
    holder = (slots // TPD).astype(jnp.int32)
    alive_mask = ((slots % TPD) < tile_count[holder]).astype(jnp.float32)
    ray_block = (tile_dest * RBD + slot_block[tile_dest, holder]).astype(jnp.int32)
    voxel_index = (holder * VBD + tile_voxel).astype(jnp.int32)
    tile_groups = tiles.reshape(N_DOM, TPD, TILE, TILE)
    inputs = (tile_groups, voxel_index.reshape(N_DOM, TPD), ray_block.reshape(N_DOM, TPD), alive_mask.reshape(N_DOM, TPD))

    def forward(running, item):
        group, voxels, blocks, alive = item
        picked = voxels_low[voxels].astype(jnp.float32)
        products = jnp.einsum('tab,tbs->tas', group.astype(jnp.float32), picked)
        products = products * alive[:, None, None]
        return running + jax.ops.segment_sum(products, blocks, num_segments=RAYBLK), None

    sinogram, _ = lax.scan(forward, jnp.zeros((RAYBLK, TILE, SLICES), jnp.float32), inputs)
    measured = jnp.log(flux / counts.astype(jnp.float32))
    residual = (sinogram - measured).astype(jnp.bfloat16)

    def backward(running, item):
        group, voxels, blocks, alive = item
        fetched = residual[blocks].astype(jnp.float32)
        products = jnp.einsum('tab,tas->tbs', group.astype(jnp.float32), fetched)
        products = products * alive[:, None, None]
        return running + jax.ops.segment_sum(products, voxels, num_segments=VOXBLK), None

    gradient, _ = lax.scan(backward, jnp.zeros((VOXBLK, TILE, SLICES), jnp.float32), inputs)
    updated = jnp.maximum(volume - step_size * gradient, 0.0)
    return updated, residual
```

```python
import functools

import jax
import jax.numpy as jnp
from jax import lax
from jax.experimental import pallas as pl
from jax.experimental.pallas import tpu as pltpu
from jax.sharding import PartitionSpec as P

flux = 32768.0
step_size = 0.5
PHASES = 2
LOADS = 4
UNROLL = 8
MAIN_VMEM = 58 * 1024 * 1024
FINISH_VMEM = 10 * 1024 * 1024
VMEM_BUDGET = 18 * 1024 * 1024
MESH = pl.DeviceIdType.MESH


def round_up(x, m):
    return (x + m - 1) // m * m


def peer_masks(n):
    chips = n // 2
    far_first = sorted(range(1, chips), key=lambda k: (k.bit_length() != (chips - 1).bit_length(), k))
    masks = []
    for k in far_first:
        masks += [2 * k, 2 * k + 1]
    return masks + [1, 0]


def dot(a, b, dims=((1,), (0,))):
    return lax.dot_general(a, b, (dims, ((), ())), preferred_element_type=jnp.float32)


def plan_lists(count, dest, voxel, order, blocks, pairs, plan_ref):
    slots = dest.shape[1]
    width = plan_ref.shape[1]
    n = len(order)
    buckets = n * blocks
    low = jnp.bfloat16
    rank = jnp.zeros_like(dest)
    for k in range(1, n):
        rank = jnp.where(dest == order[k], k, rank)
    lane = lax.broadcasted_iota(jnp.int32, (1, slots), 1)
    key = jnp.where(lane < count, rank * blocks + voxel, -1)
    b = lax.broadcasted_iota(jnp.int32, (buckets, slots), 0)
    member = key == b
    hot = member.astype(jnp.float32)
    hot_low = hot.astype(low)
    i = lax.broadcasted_iota(jnp.int32, (slots, slots), 0)
    j = lax.broadcasted_iota(jnp.int32, (slots, slots), 1)
    before = dot(hot_low, (i < j).astype(jnp.float32).astype(low))
    half = jnp.floor((jnp.sum(hot, axis=1, keepdims=True) + 1.0) * 0.5)
    row_count = dot(jnp.ones((8, slots), low), hot_low, ((1,), (1,)))
    row_half = jnp.floor((row_count + 1.0) * 0.5)
    bi = lax.broadcasted_iota(jnp.int32, (buckets, buckets), 0)
    bj = lax.broadcasted_iota(jnp.int32, (buckets, buckets), 1)
    upper = (bi < bj).astype(jnp.float32).astype(low)
    lower = (bj < bi).astype(jnp.float32).astype(low)
    row_off = dot(row_half.astype(low), upper)
    off = dot(lower, jnp.broadcast_to(half, (buckets, 128)).astype(low))[:, :1]
    place = jnp.sum(jnp.where(member, before + 2.0 * off, 0.0), axis=0, keepdims=True)
    place = jnp.where(key < 0, -1, place.astype(jnp.int32))
    p = lax.broadcasted_iota(jnp.int32, (width, slots), 0)
    chosen = (place == p).astype(jnp.float32).astype(low)
    r = lax.broadcasted_iota(jnp.int32, (8, slots), 0)
    t = lax.broadcasted_iota(jnp.int32, (8, slots), 1)
    digits = jnp.where(r == 0, t // 16, jnp.where(r == 1, t % 16, 1)).astype(jnp.float32).astype(low)
    found = dot(digits, chosen, ((1,), (1,)))
    tile = found[0:1] * 16.0 + found[1:2] + (1.0 - found[2:3]) * float(slots)
    plan_ref[0:1, :] = jnp.clip(tile.astype(jnp.int32), 0, slots)
    slot = lax.broadcasted_iota(jnp.int32, (buckets, width), 1)
    starts = jnp.where((off.astype(jnp.int32) == slot) & (half > 0.0), 1.0, 0.0)
    plan_ref[1:2, :] = jnp.sum(starts, axis=0, keepdims=True).astype(jnp.int32)
    last = jnp.where(row_half > 0.0, row_off + row_half - 1.0, float(pairs))
    plan_ref[2:3, 0:buckets] = jnp.clip(last[0:1].astype(jnp.int32), 0, pairs)


def main_kernel(n, count_hbm, dest_hbm, voxel_hbm, slot_hbm, volume_hbm, counts_hbm, tiles_hbm, *refs):
    (part_ref, last_w, last_land, residual_ref), scratch = refs[:4], refs[4:]
    bufs, stores, scratch = scratch[:PHASES], scratch[PHASES:2 * PHASES], scratch[2 * PHASES:]
    (count_ref, slot_ref, plan_s, dest_ref, voxel_ref, plan_ref, volume_ref, counts_ref, low, measured,
     out_buf, in_buf, answer_buf, landing, wt_ref, small_sems, tile_sems,
     out_send, out_recv, back_send, back_recv) = scratch
    me = lax.axis_index("dom")
    slots = tiles_hbm.shape[0]
    blocks, rows, lanes = volume_ref.shape
    owned = counts_ref.shape[0]
    step = rows // PHASES
    pairs = stores[0].shape[0] - 1
    masks = peer_masks(n)
    order = [me ^ m for m in masks]
    half = n // 2
    group = slots // LOADS

    barrier = pltpu.get_barrier_semaphore()
    for peer in order[:-1]:
        pl.semaphore_signal(barrier, inc=1, device_id={"dom": peer}, device_id_type=MESH)

    small = [
        pltpu.make_async_copy(src, dst, small_sems.at[i])
        for i, (src, dst) in enumerate((
            (count_hbm, count_ref), (dest_hbm, dest_ref), (voxel_hbm, voxel_ref), (slot_hbm, slot_ref),
            (volume_hbm, volume_ref), (counts_hbm, counts_ref)))
    ]

    def fetch(p, g):
        at = pl.ds(g * group, group)
        return pltpu.make_async_copy(
            tiles_hbm.at[at, pl.ds(p * step, step)], bufs[p].at[at], tile_sems.at[p, g])

    for copy in small[:5]:
        copy.start()
    for g in range(LOADS):
        fetch(0, g).start()
    small[5].start()
    for p in range(1, PHASES):
        for g in range(LOADS):
            fetch(p, g).start()

    for copy in small[:4]:
        copy.wait()
    plan_ref[...] = jnp.zeros_like(plan_ref)
    plan_lists(count_ref[0, 0], dest_ref[...], voxel_ref[...], order, blocks, pairs, plan_ref)
    to_smem = pltpu.make_async_copy(plan_ref, plan_s, small_sems.at[6])
    to_smem.start()

    for p in range(PHASES):
        bufs[p][slots] = jnp.zeros((step, rows), jnp.bfloat16)
        stores[p][pairs] = jnp.zeros((step, rows), jnp.bfloat16)
    small[4].wait()
    for v in range(blocks):
        low[v * rows:(v + 1) * rows, :] = volume_ref[v].astype(jnp.bfloat16)
    small[5].wait()
    for b in range(owned):
        measured[b] = jnp.log(flux / counts_ref[b].astype(jnp.float32))
    to_smem.wait()

    def fold(p):
        buf, store = bufs[p], stores[p]

        def body(j, total):
            pair = buf[plan_s[0, 2 * j]].astype(jnp.float32) + buf[plan_s[0, 2 * j + 1]].astype(jnp.float32)
            total = jnp.where(plan_s[1, j] == 1, pair, total + pair)
            store[j] = total.astype(jnp.bfloat16)
            return total

        lax.fori_loop(0, pairs, body, jnp.zeros((step, rows), jnp.float32), unroll=UNROLL)

    def summed(p, k, v):
        return stores[p][plan_s[2, k * blocks + v]]

    def project(p, k):
        w = jnp.concatenate([summed(p, k, v) for v in range(blocks)], axis=1)
        return dot(w, low[...]).astype(jnp.bfloat16)

    def transposed(p, side, v):
        w = jnp.concatenate([summed(p, side * half + k, v) for k in range(half)], axis=0)
        return w.T

    def send(src, dst, send_sems, recv_sems, p, k):
        return pltpu.make_async_remote_copy(
            src_ref=src.at[p, k], dst_ref=dst.at[p, k], send_sem=send_sems.at[p, k], recv_sem=recv_sems.at[p, k],
            device_id={"dom": order[k]}, device_id_type=MESH)

    def out(p, k):
        return send(out_buf, in_buf, out_send, out_recv, p, k)

    def back(p, k):
        return send(answer_buf, landing, back_send, back_recv, p, k)

    for p in range(PHASES):
        for g in range(LOADS):
            fetch(p, g).wait()
        fold(p)
        for k in range(n - 1):
            out_buf[p, k] = project(p, k)
            if p == 0 and k == 0:
                pl.semaphore_wait(barrier, n - 1)
            out(p, k).start()
        in_buf[p, n - 1] = project(p, n - 1)

    slot_of = [slot_ref[0, peer] for peer in order]
    for p in range(PHASES):
        for side in range(2):
            for v in range(blocks):
                if p == PHASES - 1 and side == 0:
                    last_w[v] = transposed(p, side, v)
                else:
                    wt_ref[2 * p + 1 - side, v] = transposed(p, side, v)
        for k in reversed(range(n - 1)):
            out(p, k).wait_recv()
        at = slice(p * step, (p + 1) * step)
        for b in range(owned):
            total = jnp.zeros((step, lanes), jnp.float32)
            for k in range(n):
                total += jnp.where(slot_of[k] == b, in_buf[p, k].astype(jnp.float32), 0.0)
            residual_ref[b, at, :] = (total - measured[b, at, :]).astype(jnp.bfloat16)
        for k in range(n - 1):
            answer_buf[p, k] = residual_ref[slot_of[k], at, :]
            back(p, k).start()
        landing[p, n - 1] = residual_ref[slot_of[n - 1], at, :]

    for p in range(PHASES):
        for side in (1, 0):
            for k in range(side * half, side * half + half):
                if k < n - 1:
                    back(p, k).wait_recv()
            held = landing[p, side * half:(side + 1) * half].reshape(half * step, lanes)
            if p == PHASES - 1 and side == 0:
                last_land[...] = held
                continue
            for v in range(blocks):
                base = volume_ref[v] if p == 0 and side == 1 else part_ref[v]
                part_ref[v] = base - step_size * dot(wt_ref[2 * p + 1 - side, v], held)
    for p in range(PHASES):
        for k in range(n - 1):
            out(p, k).wait_send()
            back(p, k).wait_send()


def finish_kernel(part_ref, w_ref, land_ref, residual_ref, updated_hbm, residual_hbm, updated, sems):
    blocks = part_ref.shape[0]
    copies = [pltpu.make_async_copy(residual_ref, residual_hbm, sems.at[blocks])]
    copies[0].start()
    for v in range(blocks):
        updated[v] = jnp.maximum(part_ref[v] - step_size * dot(w_ref[v], land_ref[...]), 0.0)
        copies.append(pltpu.make_async_copy(updated.at[v], updated_hbm.at[v], sems.at[v]))
        copies[-1].start()
    for copy in copies:
        copy.wait()


def fused(tiles, volume, tile_voxel, tile_dest, slot_block, tile_count, counts):
    n = lax.axis_size("dom")
    slots, rows, cols = tiles.shape
    blocks, _, lanes = volume.shape
    buckets = n * blocks
    pairs = round_up((slots + buckets + 1) // 2, UNROLL)
    width = round_up(2 * pairs, 128)
    step = rows // PHASES
    half = n // 2
    vmem = pl.BlockSpec(memory_space=pltpu.VMEM)
    hbm = pl.BlockSpec(memory_space=pltpu.HBM)
    low = jnp.bfloat16
    blocks_of = (PHASES, n, step, lanes)
    handed = pl.pallas_call(
        functools.partial(main_kernel, n),
        out_shape=(
            pltpu.VMEM(volume.shape, jnp.float32),
            pltpu.VMEM((blocks, cols, half * step), low),
            pltpu.VMEM((half * step, lanes), low),
            pltpu.VMEM(counts.shape, low),
        ),
        in_specs=[hbm] * 7,
        out_specs=(vmem,) * 4,
        scratch_shapes=[pltpu.VMEM((slots + 1, step, cols), low)] * PHASES
        + [pltpu.VMEM((pairs + 1, step, cols), low)] * PHASES
        + [
            pltpu.SMEM((1, 1), jnp.int32),
            pltpu.SMEM(slot_block.shape, jnp.int32),
            pltpu.SMEM((8, width), jnp.int32),
            pltpu.VMEM((1, slots), jnp.int32),
            pltpu.VMEM((1, slots), jnp.int32),
            pltpu.VMEM((8, width), jnp.int32),
            pltpu.VMEM(volume.shape, jnp.float32),
            pltpu.VMEM(counts.shape, jnp.int32),
            pltpu.VMEM((blocks * cols, lanes), low),
            pltpu.VMEM(counts.shape, jnp.float32),
        ]
        + [pltpu.VMEM(blocks_of, low)] * 4
        + [
            pltpu.VMEM((2 * PHASES - 1, blocks, cols, half * step), low),
            pltpu.SemaphoreType.DMA((7,)),
            pltpu.SemaphoreType.DMA((PHASES, LOADS)),
        ]
        + [pltpu.SemaphoreType.DMA((PHASES, n))] * 4,
        compiler_params=pltpu.CompilerParams(
            collective_id=0, has_side_effects=True, vmem_limit_bytes=MAIN_VMEM),
        name="exchange",
    )(tile_count.reshape(1, 1), tile_dest.reshape(1, slots), tile_voxel.reshape(1, slots), slot_block, volume, counts, tiles)
    return pl.pallas_call(
        finish_kernel,
        out_shape=(
            jax.ShapeDtypeStruct(volume.shape, jnp.float32),
            jax.ShapeDtypeStruct(counts.shape, low),
        ),
        in_specs=[vmem] * 4,
        out_specs=(hbm, hbm),
        scratch_shapes=[
            pltpu.VMEM(volume.shape, jnp.float32),
            pltpu.SemaphoreType.DMA((blocks + 1,)),
        ],
        compiler_params=pltpu.CompilerParams(vmem_limit_bytes=FINISH_VMEM),
        name="finish",
    )(*handed)


def general(tiles, volume, tile_voxel, tile_dest, slot_block, tile_count, counts):
    n = lax.axis_size("dom")
    slots, rows, cols = tiles.shape
    blocks, _, lanes = volume.shape
    low = jnp.bfloat16
    alive = jnp.arange(slots, dtype=jnp.int32) < tile_count[0]
    bucket = jnp.where(alive, tile_dest * blocks + tile_voxel, -1)
    hot = (bucket[None, :] == jnp.arange(n * blocks, dtype=jnp.int32)[:, None]).astype(low)
    w = jnp.einsum("gt,tab->gab", hot, tiles, preferred_element_type=jnp.float32).astype(low)
    w = w.reshape(n, blocks, rows, cols)
    outgoing = jnp.einsum("dvab,vbs->das", w, volume.astype(low), preferred_element_type=jnp.float32)
    incoming = lax.all_to_all(outgoing.astype(low), "dom", split_axis=0, concat_axis=0, tiled=True)
    owner = (slot_block[0][None, :] == jnp.arange(counts.shape[0], dtype=jnp.int32)[:, None]).astype(low)
    sinogram = jnp.einsum("bd,das->bas", owner, incoming, preferred_element_type=jnp.float32)
    measured = jnp.log(flux / counts.astype(jnp.float32))
    residual = (sinogram - measured).astype(low)
    answers = jnp.einsum("bd,bas->das", owner, residual, preferred_element_type=jnp.float32).astype(low)
    returned = lax.all_to_all(answers, "dom", split_axis=0, concat_axis=0, tiled=True)
    gradient = jnp.einsum("dvab,das->vbs", w, returned, preferred_element_type=jnp.float32)
    return jnp.maximum(volume - step_size * gradient, 0.0), residual


def on_device(tiles, volume, *rest):
    n = lax.axis_size("dom")
    slots, rows, cols = tiles.shape
    need = tiles.size * 2 + n * volume.shape[0] * rows * cols * 6
    if need > VMEM_BUDGET or n & (n - 1) or n < 4 or slots % LOADS or rows != cols or rows % (16 * PHASES):
        return general(tiles, volume, *rest)
    return fused(tiles, volume, *rest)


def solution(mesh):
    both = P(("slab", "dom"), None, None)
    in_specs = (P("dom", None, None), both, P("dom"), P("dom"), P("dom", None), P("dom"), both)
    return jax.shard_map(on_device, mesh=mesh, in_specs=in_specs, out_specs=(both, both), check_vma=False)
```

```python
import functools

import jax
import jax.numpy as jnp
from jax import lax
from jax.experimental import pallas as pl
from jax.experimental.pallas import tpu as pltpu
from jax.sharding import PartitionSpec as P

flux = 32768.0
step_size = 0.5
PHASES = 2
LOADS = 4
UNROLL = 8
MAIN_VMEM = 58 * 1024 * 1024
FINISH_VMEM = 10 * 1024 * 1024
VMEM_BUDGET = 18 * 1024 * 1024
MESH = pl.DeviceIdType.MESH


def round_up(x, m):
    return (x + m - 1) // m * m


def peer_masks(n):
    chips = n // 2
    far_first = sorted(range(1, chips), key=lambda k: (k.bit_length() != (chips - 1).bit_length(), k))
    masks = []
    for k in far_first:
        masks += [2 * k, 2 * k + 1]
    return masks + [1, 0]


def dot(a, b, dims=((1,), (0,))):
    return lax.dot_general(a, b, (dims, ((), ())), preferred_element_type=jnp.float32)


def plan_lists(count, dest, voxel, order, blocks, pairs, plan_ref):
    slots = dest.shape[1]
    width = plan_ref.shape[1]
    n = len(order)
    buckets = n * blocks
    low = jnp.bfloat16
    rank = jnp.zeros_like(dest)
    for k in range(1, n):
        rank = jnp.where(dest == order[k], k, rank)
    lane = lax.broadcasted_iota(jnp.int32, (1, slots), 1)
    key = jnp.where(lane < count, rank * blocks + voxel, -1)
    b = lax.broadcasted_iota(jnp.int32, (buckets, slots), 0)
    member = key == b
    hot = member.astype(jnp.float32)
    hot_low = hot.astype(low)
    i = lax.broadcasted_iota(jnp.int32, (slots, slots), 0)
    j = lax.broadcasted_iota(jnp.int32, (slots, slots), 1)
    before = dot(hot_low, (i < j).astype(jnp.float32).astype(low))
    half = jnp.floor((jnp.sum(hot, axis=1, keepdims=True) + 1.0) * 0.5)
    row_count = dot(jnp.ones((8, slots), low), hot_low, ((1,), (1,)))
    row_half = jnp.floor((row_count + 1.0) * 0.5)
    bi = lax.broadcasted_iota(jnp.int32, (buckets, buckets), 0)
    bj = lax.broadcasted_iota(jnp.int32, (buckets, buckets), 1)
    upper = (bi < bj).astype(jnp.float32).astype(low)
    lower = (bj < bi).astype(jnp.float32).astype(low)
    row_off = dot(row_half.astype(low), upper)
    off = dot(lower, jnp.broadcast_to(half, (buckets, 128)).astype(low))[:, :1]
    place = jnp.sum(jnp.where(member, before + 2.0 * off, 0.0), axis=0, keepdims=True)
    place = jnp.where(key < 0, -1, place.astype(jnp.int32))
    p = lax.broadcasted_iota(jnp.int32, (width, slots), 0)
    chosen = (place == p).astype(jnp.float32).astype(low)
    r = lax.broadcasted_iota(jnp.int32, (8, slots), 0)
    t = lax.broadcasted_iota(jnp.int32, (8, slots), 1)
    digits = jnp.where(r == 0, t // 16, jnp.where(r == 1, t % 16, 1)).astype(jnp.float32).astype(low)
    found = dot(digits, chosen, ((1,), (1,)))
    tile = found[0:1] * 16.0 + found[1:2] + (1.0 - found[2:3]) * float(slots)
    plan_ref[0:1, :] = jnp.clip(tile.astype(jnp.int32), 0, slots)
    slot = lax.broadcasted_iota(jnp.int32, (buckets, width), 1)
    starts = jnp.where((off.astype(jnp.int32) == slot) & (half > 0.0), 1.0, 0.0)
    plan_ref[1:2, :] = jnp.sum(starts, axis=0, keepdims=True).astype(jnp.int32)
    last = jnp.where(row_half > 0.0, row_off + row_half - 1.0, float(pairs))
    plan_ref[2:3, 0:buckets] = jnp.clip(last[0:1].astype(jnp.int32), 0, pairs)


def main_kernel(n, count_ref, dest_hbm, voxel_hbm, slot_hbm, volume_hbm, counts_hbm, tiles_hbm, *refs):
    (part_ref, last_w, last_land, residual_ref), scratch = refs[:4], refs[4:]
    bufs, stores, scratch = scratch[:PHASES], scratch[PHASES:2 * PHASES], scratch[2 * PHASES:]
    (slot_ref, plan_s, dest_ref, voxel_ref, plan_ref, volume_ref, counts_ref, low, measured,
     out_buf, in_buf, answer_buf, landing, wt_ref, small_sems, tile_sems,
     out_send, out_recv, back_send, back_recv) = scratch
    me = lax.axis_index("dom")
    slots = tiles_hbm.shape[0]
    blocks, rows, lanes = volume_ref.shape
    owned = counts_ref.shape[0]
    step = rows // PHASES
    pairs = stores[0].shape[0] - 1
    masks = peer_masks(n)
    order = [me ^ m for m in masks]
    half = n // 2
    group = slots // LOADS

    barrier = pltpu.get_barrier_semaphore()
    for peer in order[:-1]:
        pl.semaphore_signal(barrier, inc=1, device_id={"dom": peer}, device_id_type=MESH)

    small = [
        pltpu.make_async_copy(src, dst, small_sems.at[i])
        for i, (src, dst) in enumerate((
            (dest_hbm, dest_ref), (voxel_hbm, voxel_ref), (slot_hbm, slot_ref),
            (volume_hbm, volume_ref), (counts_hbm, counts_ref)))
    ]

    def fetch(p, g):
        at = pl.ds(g * group, group)
        return pltpu.make_async_copy(
            tiles_hbm.at[at, pl.ds(p * step, step)], bufs[p].at[at], tile_sems.at[p, g])

    for copy in small[:4]:
        copy.start()
    for g in range(LOADS):
        fetch(0, g).start()
    small[4].start()
    for p in range(1, PHASES):
        for g in range(LOADS):
            fetch(p, g).start()

    for copy in small[:3]:
        copy.wait()
    plan_ref[...] = jnp.zeros_like(plan_ref)
    plan_lists(count_ref[0], dest_ref[...].reshape(1, slots), voxel_ref[...].reshape(1, slots), order, blocks, pairs, plan_ref)
    to_smem = pltpu.make_async_copy(plan_ref, plan_s, small_sems.at[5])
    to_smem.start()

    for p in range(PHASES):
        bufs[p][slots] = jnp.zeros((step, rows), jnp.bfloat16)
        stores[p][pairs] = jnp.zeros((step, rows), jnp.bfloat16)
    small[3].wait()
    for v in range(blocks):
        low[v * rows:(v + 1) * rows, :] = volume_ref[v].astype(jnp.bfloat16)
    small[4].wait()
    for b in range(owned):
        measured[b] = jnp.log(flux / counts_ref[b].astype(jnp.float32))
    to_smem.wait()

    def fold(p):
        buf, store = bufs[p], stores[p]

        def body(j, total):
            pair = buf[plan_s[0, 2 * j]].astype(jnp.float32) + buf[plan_s[0, 2 * j + 1]].astype(jnp.float32)
            total = jnp.where(plan_s[1, j] == 1, pair, total + pair)
            store[j] = total.astype(jnp.bfloat16)
            return total

        lax.fori_loop(0, pairs, body, jnp.zeros((step, rows), jnp.float32), unroll=UNROLL)

    def summed(p, k, v):
        return stores[p][plan_s[2, k * blocks + v]]

    def project(p, k):
        w = jnp.concatenate([summed(p, k, v) for v in range(blocks)], axis=1)
        return dot(w, low[...]).astype(jnp.bfloat16)

    def transposed(p, side, v):
        w = jnp.concatenate([summed(p, side * half + k, v) for k in range(half)], axis=0)
        return w.T

    def send(src, dst, send_sems, recv_sems, p, k):
        return pltpu.make_async_remote_copy(
            src_ref=src.at[p, k], dst_ref=dst.at[p, k], send_sem=send_sems.at[p, k], recv_sem=recv_sems.at[p, k],
            device_id={"dom": order[k]}, device_id_type=MESH)

    def out(p, k):
        return send(out_buf, in_buf, out_send, out_recv, p, k)

    def back(p, k):
        return send(answer_buf, landing, back_send, back_recv, p, k)

    for p in range(PHASES):
        for g in range(LOADS):
            fetch(p, g).wait()
        fold(p)
        for k in range(n - 1):
            out_buf[p, k] = project(p, k)
            if p == 0 and k == 0:
                pl.semaphore_wait(barrier, n - 1)
            out(p, k).start()
        in_buf[p, n - 1] = project(p, n - 1)

    slot_of = [slot_ref[0, peer] for peer in order]
    for p in range(PHASES):
        for side in range(2):
            for v in range(blocks):
                if p == PHASES - 1 and side == 0:
                    last_w[v] = transposed(p, side, v)
                else:
                    wt_ref[2 * p + 1 - side, v] = transposed(p, side, v)
        for k in reversed(range(n - 1)):
            out(p, k).wait_recv()
        at = slice(p * step, (p + 1) * step)
        for b in range(owned):
            total = jnp.zeros((step, lanes), jnp.float32)
            for k in range(n):
                total += jnp.where(slot_of[k] == b, in_buf[p, k].astype(jnp.float32), 0.0)
            residual_ref[b, at, :] = (total - measured[b, at, :]).astype(jnp.bfloat16)
        for k in range(n - 1):
            answer_buf[p, k] = residual_ref[slot_of[k], at, :]
            back(p, k).start()
        landing[p, n - 1] = residual_ref[slot_of[n - 1], at, :]

    for p in range(PHASES):
        for side in (1, 0):
            for k in range(side * half, side * half + half):
                if k < n - 1:
                    back(p, k).wait_recv()
            held = landing[p, side * half:(side + 1) * half].reshape(half * step, lanes)
            if p == PHASES - 1 and side == 0:
                last_land[...] = held
                continue
            for v in range(blocks):
                base = volume_ref[v] if p == 0 and side == 1 else part_ref[v]
                part_ref[v] = base - step_size * dot(wt_ref[2 * p + 1 - side, v], held)
    for p in range(PHASES):
        for k in range(n - 1):
            out(p, k).wait_send()
            back(p, k).wait_send()


def finish_kernel(part_ref, w_ref, land_ref, residual_ref, updated_hbm, residual_hbm, updated, sems):
    blocks = part_ref.shape[0]
    copies = [pltpu.make_async_copy(residual_ref, residual_hbm, sems.at[blocks])]
    copies[0].start()
    for v in range(blocks):
        updated[v] = jnp.maximum(part_ref[v] - step_size * dot(w_ref[v], land_ref[...]), 0.0)
        copies.append(pltpu.make_async_copy(updated.at[v], updated_hbm.at[v], sems.at[v]))
        copies[-1].start()
    for copy in copies:
        copy.wait()


def fused(tiles, volume, tile_voxel, tile_dest, slot_block, tile_count, counts):
    n = lax.axis_size("dom")
    slots, rows, cols = tiles.shape
    blocks, _, lanes = volume.shape
    buckets = n * blocks
    pairs = round_up((slots + buckets + 1) // 2, UNROLL)
    width = round_up(2 * pairs, 128)
    step = rows // PHASES
    half = n // 2
    vmem = pl.BlockSpec(memory_space=pltpu.VMEM)
    hbm = pl.BlockSpec(memory_space=pltpu.HBM)
    low = jnp.bfloat16
    blocks_of = (PHASES, n, step, lanes)
    handed = pl.pallas_call(
        functools.partial(main_kernel, n),
        out_shape=(
            pltpu.VMEM(volume.shape, jnp.float32),
            pltpu.VMEM((blocks, cols, half * step), low),
            pltpu.VMEM((half * step, lanes), low),
            pltpu.VMEM(counts.shape, low),
        ),
        in_specs=[pl.BlockSpec(memory_space=pltpu.SMEM)] + [hbm] * 6,
        out_specs=(vmem,) * 4,
        scratch_shapes=[pltpu.VMEM((slots + 1, step, cols), low)] * PHASES
        + [pltpu.VMEM((pairs + 1, step, cols), low)] * PHASES
        + [
            pltpu.SMEM(slot_block.shape, jnp.int32),
            pltpu.SMEM((8, width), jnp.int32),
            pltpu.VMEM((slots,), jnp.int32),
            pltpu.VMEM((slots,), jnp.int32),
            pltpu.VMEM((8, width), jnp.int32),
            pltpu.VMEM(volume.shape, jnp.float32),
            pltpu.VMEM(counts.shape, jnp.int32),
            pltpu.VMEM((blocks * cols, lanes), low),
            pltpu.VMEM(counts.shape, jnp.float32),
        ]
        + [pltpu.VMEM(blocks_of, low)] * 4
        + [
            pltpu.VMEM((2 * PHASES - 1, blocks, cols, half * step), low),
            pltpu.SemaphoreType.DMA((7,)),
            pltpu.SemaphoreType.DMA((PHASES, LOADS)),
        ]
        + [pltpu.SemaphoreType.DMA((PHASES, n))] * 4,
        compiler_params=pltpu.CompilerParams(
            collective_id=0, has_side_effects=True, vmem_limit_bytes=MAIN_VMEM),
        name="exchange",
    )(tile_count, tile_dest, tile_voxel, slot_block, volume, counts, tiles)
    return pl.pallas_call(
        finish_kernel,
        out_shape=(
            jax.ShapeDtypeStruct(volume.shape, jnp.float32),
            jax.ShapeDtypeStruct(counts.shape, low),
        ),
        in_specs=[vmem] * 4,
        out_specs=(hbm, hbm),
        scratch_shapes=[
            pltpu.VMEM(volume.shape, jnp.float32),
            pltpu.SemaphoreType.DMA((blocks + 1,)),
        ],
        compiler_params=pltpu.CompilerParams(vmem_limit_bytes=FINISH_VMEM),
        name="finish",
    )(*handed)


def general(tiles, volume, tile_voxel, tile_dest, slot_block, tile_count, counts):
    n = lax.axis_size("dom")
    slots, rows, cols = tiles.shape
    blocks, _, lanes = volume.shape
    low = jnp.bfloat16
    alive = jnp.arange(slots, dtype=jnp.int32) < tile_count[0]
    bucket = jnp.where(alive, tile_dest * blocks + tile_voxel, -1)
    hot = (bucket[None, :] == jnp.arange(n * blocks, dtype=jnp.int32)[:, None]).astype(low)
    w = jnp.einsum("gt,tab->gab", hot, tiles, preferred_element_type=jnp.float32).astype(low)
    w = w.reshape(n, blocks, rows, cols)
    outgoing = jnp.einsum("dvab,vbs->das", w, volume.astype(low), preferred_element_type=jnp.float32)
    incoming = lax.all_to_all(outgoing.astype(low), "dom", split_axis=0, concat_axis=0, tiled=True)
    owner = (slot_block[0][None, :] == jnp.arange(counts.shape[0], dtype=jnp.int32)[:, None]).astype(low)
    sinogram = jnp.einsum("bd,das->bas", owner, incoming, preferred_element_type=jnp.float32)
    measured = jnp.log(flux / counts.astype(jnp.float32))
    residual = (sinogram - measured).astype(low)
    answers = jnp.einsum("bd,bas->das", owner, residual, preferred_element_type=jnp.float32).astype(low)
    returned = lax.all_to_all(answers, "dom", split_axis=0, concat_axis=0, tiled=True)
    gradient = jnp.einsum("dvab,das->vbs", w, returned, preferred_element_type=jnp.float32)
    return jnp.maximum(volume - step_size * gradient, 0.0), residual


def on_device(tiles, volume, *rest):
    n = lax.axis_size("dom")
    slots, rows, cols = tiles.shape
    need = tiles.size * 2 + n * volume.shape[0] * rows * cols * 6
    if need > VMEM_BUDGET or n & (n - 1) or n < 4 or slots % LOADS or rows != cols or rows % (16 * PHASES):
        return general(tiles, volume, *rest)
    return fused(tiles, volume, *rest)


def solution(mesh):
    both = P(("slab", "dom"), None, None)
    in_specs = (P("dom", None, None), both, P("dom"), P("dom"), P("dom", None), P("dom"), both)
    return jax.shard_map(on_device, mesh=mesh, in_specs=in_specs, out_specs=(both, both), check_vma=False)
```

```python
import functools

import jax
import jax.numpy as jnp
from jax import lax
from jax.experimental import pallas as pl
from jax.experimental.pallas import tpu as pltpu
from jax.sharding import PartitionSpec as P

flux = 32768.0
step_size = 0.5
PHASES = 4
LOADS = 5
UNROLL = 16
MAIN_VMEM = 58 * 1024 * 1024
FINISH_VMEM = 10 * 1024 * 1024
VMEM_BUDGET = 18 * 1024 * 1024
MESH = pl.DeviceIdType.MESH


def round_up(x, m):
    return (x + m - 1) // m * m


def peer_masks(n):
    chips = n // 2
    far_first = sorted(range(1, chips), key=lambda k: (k.bit_length() != (chips - 1).bit_length(), k))
    masks = []
    for k in far_first:
        masks += [2 * k, 2 * k + 1]
    return masks + [1, 0]


def dot(a, b, dims=((1,), (0,))):
    return lax.dot_general(a, b, (dims, ((), ())), preferred_element_type=jnp.float32)


def plan_lists(count, dest, voxel, order, blocks, pairs, plan_ref):
    slots = dest.shape[1]
    width = plan_ref.shape[1]
    n = len(order)
    buckets = n * blocks
    low = jnp.bfloat16
    rank = jnp.zeros_like(dest)
    for k in range(1, n):
        rank = jnp.where(dest == order[k], k, rank)
    lane = lax.broadcasted_iota(jnp.int32, (1, slots), 1)
    key = jnp.where(lane < count, rank * blocks + voxel, -1)
    b = lax.broadcasted_iota(jnp.int32, (buckets, slots), 0)
    member = key == b
    hot = member.astype(jnp.float32)
    hot_low = hot.astype(low)
    i = lax.broadcasted_iota(jnp.int32, (slots, slots), 0)
    j = lax.broadcasted_iota(jnp.int32, (slots, slots), 1)
    before = dot(hot_low, (i < j).astype(jnp.float32).astype(low))
    half = jnp.floor((jnp.sum(hot, axis=1, keepdims=True) + 1.0) * 0.5)
    row_count = dot(jnp.ones((8, slots), low), hot_low, ((1,), (1,)))
    row_half = jnp.floor((row_count + 1.0) * 0.5)
    bi = lax.broadcasted_iota(jnp.int32, (buckets, buckets), 0)
    bj = lax.broadcasted_iota(jnp.int32, (buckets, buckets), 1)
    upper = (bi < bj).astype(jnp.float32).astype(low)
    lower = (bj < bi).astype(jnp.float32).astype(low)
    row_off = dot(row_half.astype(low), upper)
    off = dot(lower, jnp.broadcast_to(half, (buckets, 128)).astype(low))[:, :1]
    place = jnp.sum(jnp.where(member, before + 2.0 * off, 0.0), axis=0, keepdims=True)
    place = jnp.where(key < 0, -1, place.astype(jnp.int32))
    p = lax.broadcasted_iota(jnp.int32, (width, slots), 0)
    chosen = (place == p).astype(jnp.float32).astype(low)
    r = lax.broadcasted_iota(jnp.int32, (8, slots), 0)
    t = lax.broadcasted_iota(jnp.int32, (8, slots), 1)
    digits = jnp.where(r == 0, t // 16, jnp.where(r == 1, t % 16, 1)).astype(jnp.float32).astype(low)
    found = dot(digits, chosen, ((1,), (1,)))
    tile = found[0:1] * 16.0 + found[1:2] + (1.0 - found[2:3]) * float(slots)
    plan_ref[0:1, :] = jnp.clip(tile.astype(jnp.int32), 0, slots)
    slot = lax.broadcasted_iota(jnp.int32, (buckets, width), 1)
    starts = jnp.where((off.astype(jnp.int32) == slot) & (half > 0.0), 1.0, 0.0)
    plan_ref[1:2, :] = jnp.sum(starts, axis=0, keepdims=True).astype(jnp.int32)
    last = jnp.where(row_half > 0.0, row_off + row_half - 1.0, float(pairs))
    plan_ref[2:3, 0:buckets] = jnp.clip(last[0:1].astype(jnp.int32), 0, pairs)


def main_kernel(n, count_ref, dest_hbm, voxel_hbm, slot_hbm, volume_hbm, counts_hbm, tiles_hbm, *refs):
    (part_ref, last_w, last_land, residual_ref), scratch = refs[:4], refs[4:]
    bufs, stores, scratch = scratch[:PHASES], scratch[PHASES:2 * PHASES], scratch[2 * PHASES:]
    (slot_ref, plan_s, dest_ref, voxel_ref, plan_ref, volume_ref, counts_ref, low, measured,
     out_buf, in_buf, answer_buf, landing, wt_ref, small_sems, tile_sems,
     out_send, out_recv, back_send, back_recv) = scratch
    me = lax.axis_index("dom")
    slots = tiles_hbm.shape[0]
    blocks, rows, lanes = volume_ref.shape
    owned = counts_ref.shape[0]
    step = rows // PHASES
    pairs = stores[0].shape[0] - 1
    masks = peer_masks(n)
    order = [me ^ m for m in masks]
    half = n // 2
    group = slots // LOADS

    barrier = pltpu.get_barrier_semaphore()
    for peer in order[:-1]:
        pl.semaphore_signal(barrier, inc=1, device_id={"dom": peer}, device_id_type=MESH)

    small = [
        pltpu.make_async_copy(src, dst, small_sems.at[i])
        for i, (src, dst) in enumerate((
            (dest_hbm, dest_ref), (voxel_hbm, voxel_ref), (slot_hbm, slot_ref),
            (volume_hbm, volume_ref), (counts_hbm, counts_ref)))
    ]

    def fetch(p, g):
        at = pl.ds(g * group, group)
        return pltpu.make_async_copy(
            tiles_hbm.at[at, pl.ds(p * step, step)], bufs[p].at[at], tile_sems.at[p, g])

    for copy in small[:4]:
        copy.start()
    for g in range(LOADS):
        fetch(0, g).start()
    small[4].start()
    for p in range(1, PHASES):
        for g in range(LOADS):
            fetch(p, g).start()

    for copy in small[:3]:
        copy.wait()
    plan_ref[...] = jnp.zeros_like(plan_ref)
    plan_lists(count_ref[0], dest_ref[...].reshape(1, slots), voxel_ref[...].reshape(1, slots), order, blocks, pairs, plan_ref)
    to_smem = pltpu.make_async_copy(plan_ref, plan_s, small_sems.at[5])
    to_smem.start()

    for p in range(PHASES):
        bufs[p][slots] = jnp.zeros((step, rows), jnp.bfloat16)
        stores[p][pairs] = jnp.zeros((step, rows), jnp.bfloat16)
    small[3].wait()
    for v in range(blocks):
        low[v * rows:(v + 1) * rows, :] = volume_ref[v].astype(jnp.bfloat16)
    small[4].wait()
    for b in range(owned):
        measured[b] = jnp.log(flux / counts_ref[b].astype(jnp.float32))
    to_smem.wait()

    def fold(p):
        buf, store = bufs[p], stores[p]

        def body(j, total):
            pair = buf[plan_s[0, 2 * j]].astype(jnp.float32) + buf[plan_s[0, 2 * j + 1]].astype(jnp.float32)
            total = jnp.where(plan_s[1, j] == 1, pair, total + pair)
            store[j] = total.astype(jnp.bfloat16)
            return total

        lax.fori_loop(0, pairs, body, jnp.zeros((step, rows), jnp.float32), unroll=UNROLL)

    def summed(p, k, v):
        return stores[p][plan_s[2, k * blocks + v]]

    def project(p, k):
        w = jnp.concatenate([summed(p, k, v) for v in range(blocks)], axis=1)
        return dot(w, low[...]).astype(jnp.bfloat16)

    def transposed(p, side, v):
        w = jnp.concatenate([summed(p, side * half + k, v) for k in range(half)], axis=0)
        return w.T

    def send(src, dst, send_sems, recv_sems, p, k):
        return pltpu.make_async_remote_copy(
            src_ref=src.at[p, k], dst_ref=dst.at[p, k], send_sem=send_sems.at[p, k], recv_sem=recv_sems.at[p, k],
            device_id={"dom": order[k]}, device_id_type=MESH)

    def out(p, k):
        return send(out_buf, in_buf, out_send, out_recv, p, k)

    def back(p, k):
        return send(answer_buf, landing, back_send, back_recv, p, k)

    for p in range(PHASES):
        for g in range(LOADS):
            fetch(p, g).wait()
        fold(p)
        for k in range(n - 1):
            out_buf[p, k] = project(p, k)
            if p == 0 and k == 0:
                pl.semaphore_wait(barrier, n - 1)
            out(p, k).start()
        in_buf[p, n - 1] = project(p, n - 1)

    slot_of = [slot_ref[0, peer] for peer in order]
    for p in range(PHASES):
        for side in range(2):
            for v in range(blocks):
                if p == PHASES - 1 and side == 0:
                    last_w[v] = transposed(p, side, v)
                else:
                    wt_ref[2 * p + 1 - side, v] = transposed(p, side, v)
        for k in reversed(range(n - 1)):
            out(p, k).wait_recv()
        at = slice(p * step, (p + 1) * step)
        for b in range(owned):
            total = jnp.zeros((step, lanes), jnp.float32)
            for k in range(n):
                total += jnp.where(slot_of[k] == b, in_buf[p, k].astype(jnp.float32), 0.0)
            residual_ref[b, at, :] = (total - measured[b, at, :]).astype(jnp.bfloat16)
        for k in range(n - 1):
            answer_buf[p, k] = residual_ref[slot_of[k], at, :]
            back(p, k).start()
        landing[p, n - 1] = residual_ref[slot_of[n - 1], at, :]

    for p in range(PHASES):
        for side in (1, 0):
            for k in range(side * half, side * half + half):
                if k < n - 1:
                    back(p, k).wait_recv()
            held = landing[p, side * half:(side + 1) * half].reshape(half * step, lanes)
            if p == PHASES - 1 and side == 0:
                last_land[...] = held
                continue
            for v in range(blocks):
                base = volume_ref[v] if p == 0 and side == 1 else part_ref[v]
                part_ref[v] = base - step_size * dot(wt_ref[2 * p + 1 - side, v], held)
    for p in range(PHASES):
        for k in range(n - 1):
            out(p, k).wait_send()
            back(p, k).wait_send()


def finish_kernel(part_ref, w_ref, land_ref, residual_ref, updated_hbm, residual_hbm, updated, sems):
    blocks = part_ref.shape[0]
    copies = [pltpu.make_async_copy(residual_ref, residual_hbm, sems.at[blocks])]
    copies[0].start()
    for v in range(blocks):
        updated[v] = jnp.maximum(part_ref[v] - step_size * dot(w_ref[v], land_ref[...]), 0.0)
        copies.append(pltpu.make_async_copy(updated.at[v], updated_hbm.at[v], sems.at[v]))
        copies[-1].start()
    for copy in copies:
        copy.wait()


def fused(tiles, volume, tile_voxel, tile_dest, slot_block, tile_count, counts):
    n = lax.axis_size("dom")
    slots, rows, cols = tiles.shape
    blocks, _, lanes = volume.shape
    buckets = n * blocks
    pairs = round_up((slots + buckets + 1) // 2, UNROLL)
    width = round_up(2 * pairs, 128)
    step = rows // PHASES
    half = n // 2
    vmem = pl.BlockSpec(memory_space=pltpu.VMEM)
    hbm = pl.BlockSpec(memory_space=pltpu.HBM)
    low = jnp.bfloat16
    blocks_of = (PHASES, n, step, lanes)
    handed = pl.pallas_call(
        functools.partial(main_kernel, n),
        out_shape=(
            pltpu.VMEM(volume.shape, jnp.float32),
            pltpu.VMEM((blocks, cols, half * step), low),
            pltpu.VMEM((half * step, lanes), low),
            pltpu.VMEM(counts.shape, low),
        ),
        in_specs=[pl.BlockSpec(memory_space=pltpu.SMEM)] + [hbm] * 6,
        out_specs=(vmem,) * 4,
        scratch_shapes=[pltpu.VMEM((slots + 1, step, cols), low)] * PHASES
        + [pltpu.VMEM((pairs + 1, step, cols), low)] * PHASES
        + [
            pltpu.SMEM(slot_block.shape, jnp.int32),
            pltpu.SMEM((8, width), jnp.int32),
            pltpu.VMEM((slots,), jnp.int32),
            pltpu.VMEM((slots,), jnp.int32),
            pltpu.VMEM((8, width), jnp.int32),
            pltpu.VMEM(volume.shape, jnp.float32),
            pltpu.VMEM(counts.shape, jnp.int32),
            pltpu.VMEM((blocks * cols, lanes), low),
            pltpu.VMEM(counts.shape, jnp.float32),
        ]
        + [pltpu.VMEM(blocks_of, low)] * 4
        + [
            pltpu.VMEM((2 * PHASES - 1, blocks, cols, half * step), low),
            pltpu.SemaphoreType.DMA((7,)),
            pltpu.SemaphoreType.DMA((PHASES, LOADS)),
        ]
        + [pltpu.SemaphoreType.DMA((PHASES, n))] * 4,
        compiler_params=pltpu.CompilerParams(
            collective_id=0, has_side_effects=True, vmem_limit_bytes=MAIN_VMEM),
        name="exchange",
    )(tile_count, tile_dest, tile_voxel, slot_block, volume, counts, tiles)
    return pl.pallas_call(
        finish_kernel,
        out_shape=(
            jax.ShapeDtypeStruct(volume.shape, jnp.float32),
            jax.ShapeDtypeStruct(counts.shape, low),
        ),
        in_specs=[vmem] * 4,
        out_specs=(hbm, hbm),
        scratch_shapes=[
            pltpu.VMEM(volume.shape, jnp.float32),
            pltpu.SemaphoreType.DMA((blocks + 1,)),
        ],
        compiler_params=pltpu.CompilerParams(vmem_limit_bytes=FINISH_VMEM),
        name="finish",
    )(*handed)


def general(tiles, volume, tile_voxel, tile_dest, slot_block, tile_count, counts):
    n = lax.axis_size("dom")
    slots, rows, cols = tiles.shape
    blocks, _, lanes = volume.shape
    low = jnp.bfloat16
    alive = jnp.arange(slots, dtype=jnp.int32) < tile_count[0]
    bucket = jnp.where(alive, tile_dest * blocks + tile_voxel, -1)
    hot = (bucket[None, :] == jnp.arange(n * blocks, dtype=jnp.int32)[:, None]).astype(low)
    w = jnp.einsum("gt,tab->gab", hot, tiles, preferred_element_type=jnp.float32).astype(low)
    w = w.reshape(n, blocks, rows, cols)
    outgoing = jnp.einsum("dvab,vbs->das", w, volume.astype(low), preferred_element_type=jnp.float32)
    incoming = lax.all_to_all(outgoing.astype(low), "dom", split_axis=0, concat_axis=0, tiled=True)
    owner = (slot_block[0][None, :] == jnp.arange(counts.shape[0], dtype=jnp.int32)[:, None]).astype(low)
    sinogram = jnp.einsum("bd,das->bas", owner, incoming, preferred_element_type=jnp.float32)
    measured = jnp.log(flux / counts.astype(jnp.float32))
    residual = (sinogram - measured).astype(low)
    answers = jnp.einsum("bd,bas->das", owner, residual, preferred_element_type=jnp.float32).astype(low)
    returned = lax.all_to_all(answers, "dom", split_axis=0, concat_axis=0, tiled=True)
    gradient = jnp.einsum("dvab,das->vbs", w, returned, preferred_element_type=jnp.float32)
    return jnp.maximum(volume - step_size * gradient, 0.0), residual


def on_device(tiles, volume, *rest):
    n = lax.axis_size("dom")
    slots, rows, cols = tiles.shape
    need = tiles.size * 2 + n * volume.shape[0] * rows * cols * 6
    if need > VMEM_BUDGET or n & (n - 1) or n < 4 or slots % LOADS or rows != cols or rows % (16 * PHASES):
        return general(tiles, volume, *rest)
    return fused(tiles, volume, *rest)


def solution(mesh):
    both = P(("slab", "dom"), None, None)
    in_specs = (P("dom", None, None), both, P("dom"), P("dom"), P("dom", None), P("dom"), both)
    return jax.shard_map(on_device, mesh=mesh, in_specs=in_specs, out_specs=(both, both), check_vma=False)
```

```python
import functools

import jax
import jax.numpy as jnp
from jax import lax
from jax.experimental import pallas as pl
from jax.experimental.pallas import tpu as pltpu
from jax.sharding import PartitionSpec as P

flux = 32768.0
step_size = 0.5
PHASES = 2
LOADS = 4
UNROLL = 8
REPEAT = 2
MAIN_VMEM = 58 * 1024 * 1024
FINISH_VMEM = 10 * 1024 * 1024
VMEM_BUDGET = 18 * 1024 * 1024
MESH = pl.DeviceIdType.MESH


def round_up(x, m):
    return (x + m - 1) // m * m


def peer_masks(n):
    chips = n // 2
    far_first = sorted(range(1, chips), key=lambda k: (k.bit_length() != (chips - 1).bit_length(), k))
    masks = []
    for k in far_first:
        masks += [2 * k, 2 * k + 1]
    return masks + [1, 0]


def dot(a, b, dims=((1,), (0,))):
    return lax.dot_general(a, b, (dims, ((), ())), preferred_element_type=jnp.float32)


def plan_lists(count, dest, voxel, order, blocks, pairs, plan_ref):
    slots = dest.shape[1]
    width = plan_ref.shape[1]
    n = len(order)
    buckets = n * blocks
    low = jnp.bfloat16
    rank = jnp.zeros_like(dest)
    for k in range(1, n):
        rank = jnp.where(dest == order[k], k, rank)
    lane = lax.broadcasted_iota(jnp.int32, (1, slots), 1)
    key = jnp.where(lane < count, rank * blocks + voxel, -1)
    b = lax.broadcasted_iota(jnp.int32, (buckets, slots), 0)
    member = key == b
    hot = member.astype(jnp.float32)
    hot_low = hot.astype(low)
    i = lax.broadcasted_iota(jnp.int32, (slots, slots), 0)
    j = lax.broadcasted_iota(jnp.int32, (slots, slots), 1)
    before = dot(hot_low, (i < j).astype(jnp.float32).astype(low))
    half = jnp.floor((jnp.sum(hot, axis=1, keepdims=True) + 1.0) * 0.5)
    row_count = dot(jnp.ones((8, slots), low), hot_low, ((1,), (1,)))
    row_half = jnp.floor((row_count + 1.0) * 0.5)
    bi = lax.broadcasted_iota(jnp.int32, (buckets, buckets), 0)
    bj = lax.broadcasted_iota(jnp.int32, (buckets, buckets), 1)
    upper = (bi < bj).astype(jnp.float32).astype(low)
    lower = (bj < bi).astype(jnp.float32).astype(low)
    row_off = dot(row_half.astype(low), upper)
    off = dot(lower, jnp.broadcast_to(half, (buckets, 128)).astype(low))[:, :1]
    place = jnp.sum(jnp.where(member, before + 2.0 * off, 0.0), axis=0, keepdims=True)
    place = jnp.where(key < 0, -1, place.astype(jnp.int32))
    p = lax.broadcasted_iota(jnp.int32, (width, slots), 0)
    chosen = (place == p).astype(jnp.float32).astype(low)
    r = lax.broadcasted_iota(jnp.int32, (8, slots), 0)
    t = lax.broadcasted_iota(jnp.int32, (8, slots), 1)
    digits = jnp.where(r == 0, t // 16, jnp.where(r == 1, t % 16, 1)).astype(jnp.float32).astype(low)
    found = dot(digits, chosen, ((1,), (1,)))
    tile = found[0:1] * 16.0 + found[1:2] + (1.0 - found[2:3]) * float(slots)
    plan_ref[0:1, :] = jnp.clip(tile.astype(jnp.int32), 0, slots)
    slot = lax.broadcasted_iota(jnp.int32, (buckets, width), 1)
    starts = jnp.where((off.astype(jnp.int32) == slot) & (half > 0.0), 1.0, 0.0)
    plan_ref[1:2, :] = jnp.sum(starts, axis=0, keepdims=True).astype(jnp.int32)
    last = jnp.where(row_half > 0.0, row_off + row_half - 1.0, float(pairs))
    plan_ref[2:3, 0:buckets] = jnp.clip(last[0:1].astype(jnp.int32), 0, pairs)


def main_kernel(n, count_ref, dest_hbm, voxel_hbm, slot_hbm, volume_hbm, counts_hbm, tiles_hbm, *refs):
    (part_ref, last_w, last_land, residual_ref), scratch = refs[:4], refs[4:]
    bufs, stores, scratch = scratch[:PHASES], scratch[PHASES:2 * PHASES], scratch[2 * PHASES:]
    (slot_ref, list_s, fresh_s, last_s, dest_ref, voxel_ref, plan_ref, volume_ref, counts_ref, low, measured,
     out_buf, in_buf, answer_buf, landing, wt_ref, small_sems, tile_sems,
     out_send, out_recv, back_send, back_recv) = scratch
    me = lax.axis_index("dom")
    slots = tiles_hbm.shape[0]
    blocks, rows, lanes = volume_ref.shape
    owned = counts_ref.shape[0]
    step = rows // PHASES
    pairs = stores[0].shape[0] - 1
    masks = peer_masks(n)
    order = [me ^ m for m in masks]
    half = n // 2
    group = slots // LOADS
    z = me // 2
    swap = ((z + 1) // 2 + 1) % 2 * 2 if half == 4 else 0
    send_order = [[k + swap if k < 2 else k - swap for k in range(half)], list(range(half, n - 1))]

    barrier = pltpu.get_barrier_semaphore()
    for peer in order[:-1]:
        pl.semaphore_signal(barrier, inc=1, device_id={"dom": peer}, device_id_type=MESH)

    small = [
        pltpu.make_async_copy(src, dst, small_sems.at[i])
        for i, (src, dst) in enumerate((
            (dest_hbm, dest_ref), (voxel_hbm, voxel_ref), (slot_hbm, slot_ref),
            (volume_hbm, volume_ref), (counts_hbm, counts_ref)))
    ]

    def fetch(p, g):
        at = pl.ds(g * group, group)
        return pltpu.make_async_copy(
            tiles_hbm.at[at, pl.ds(p * step, step)], bufs[p].at[at], tile_sems.at[p, g])

    for copy in small[:3]:
        copy.start()
    for g in range(LOADS):
        fetch(0, g).start()
    for copy in small[3:5]:
        copy.start()
    for p in range(1, PHASES):
        for g in range(LOADS):
            fetch(p, g).start()

    for copy in small[:3]:
        copy.wait()
    plan_ref[...] = jnp.zeros_like(plan_ref)
    plan_lists(count_ref[0], dest_ref[...].reshape(1, slots), voxel_ref[...].reshape(1, slots), order, blocks, pairs, plan_ref)
    to_smem = [
        pltpu.make_async_copy(plan_ref.at[r], dst, small_sems.at[5 + r])
        for r, dst in enumerate((list_s, fresh_s, last_s))
    ]
    for copy in to_smem:
        copy.start()

    for p in range(PHASES):
        bufs[p][slots] = jnp.zeros((step, rows), jnp.bfloat16)
        stores[p][pairs] = jnp.zeros((step, rows), jnp.bfloat16)
    for copy in to_smem:
        copy.wait()

    def fold(p):
        buf, store = bufs[p], stores[p]

        def body(i, total):
            first = i * UNROLL
            tiles = [buf[list_s[2 * first + t]] for t in range(2 * UNROLL)]
            fresh = [fresh_s[first + u] == 1 for u in range(UNROLL)]
            done = []
            for u in range(UNROLL):
                pair = tiles[2 * u].astype(jnp.float32) + tiles[2 * u + 1].astype(jnp.float32)
                total = jnp.where(fresh[u], pair, total + pair)
                done.append(total.astype(jnp.bfloat16))
            for u in range(UNROLL):
                store[first + u] = done[u]
            return total

        lax.fori_loop(0, pairs // UNROLL, body, jnp.zeros((step, rows), jnp.float32), unroll=REPEAT)

    def summed(p, k, v):
        return stores[p][last_s[k * blocks + v]]

    def project(p, ks):
        w = jnp.concatenate(
            [jnp.concatenate([summed(p, k, v) for v in range(blocks)], axis=1) for k in ks], axis=0)
        return dot(w, low[...]).astype(jnp.bfloat16)

    def transposed(p, side, v):
        w = jnp.concatenate([summed(p, side * half + k, v) for k in range(half)], axis=0)
        return w.T

    def peer_of(k):
        if isinstance(k, int):
            return order[k]
        return me ^ (half + k)

    def send(src, dst, send_sems, recv_sems, p, k):
        return pltpu.make_async_remote_copy(
            src_ref=src.at[p, k], dst_ref=dst.at[p, k], send_sem=send_sems.at[p, k], recv_sem=recv_sems.at[p, k],
            device_id={"dom": peer_of(k)}, device_id_type=MESH)

    def out(p, k):
        return send(out_buf, in_buf, out_send, out_recv, p, k)

    def back(p, k):
        return send(answer_buf, landing, back_send, back_recv, p, k)

    for p in range(PHASES):
        for g in range(LOADS):
            fetch(p, g).wait()
        fold(p)
        if p == 0:
            small[3].wait()
            for v in range(blocks):
                low[v * rows:(v + 1) * rows, :] = volume_ref[v].astype(jnp.bfloat16)
        for side in range(2):
            ks = range(side * half, side * half + half)
            y = project(p, ks)
            for i, k in enumerate(ks):
                (out_buf if k < n - 1 else in_buf)[p, k] = y[i * step:(i + 1) * step]
            if p == 0 and side == 0:
                pl.semaphore_wait(barrier, n - 1)
            for k in send_order[side]:
                out(p, k).start()

    small[4].wait()
    for b in range(owned):
        measured[b] = jnp.log(flux / counts_ref[b].astype(jnp.float32))
    slot_of = [slot_ref[0, peer] for peer in order]
    for p in range(PHASES):
        for side in range(2):
            for v in range(blocks):
                if p == PHASES - 1 and side == 0:
                    last_w[v] = transposed(p, side, v)
                else:
                    wt_ref[2 * p + 1 - side, v] = transposed(p, side, v)
        for k in reversed(range(n - 1)):
            out(p, k).wait_recv()
        at = slice(p * step, (p + 1) * step)
        for b in range(owned):
            total = jnp.zeros((step, lanes), jnp.float32)
            for k in range(n):
                total += jnp.where(slot_of[k] == b, in_buf[p, k].astype(jnp.float32), 0.0)
            residual_ref[b, at, :] = (total - measured[b, at, :]).astype(jnp.bfloat16)
        for k in range(n - 1):
            answer_buf[p, k] = residual_ref[slot_of[k], at, :]
        for k in send_order[0] + send_order[1]:
            back(p, k).start()
        landing[p, n - 1] = residual_ref[slot_of[n - 1], at, :]

    for p in range(PHASES):
        for side in (1, 0):
            for k in range(side * half, side * half + half):
                if k < n - 1:
                    back(p, k).wait_recv()
            held = landing[p, side * half:(side + 1) * half].reshape(half * step, lanes)
            if p == PHASES - 1 and side == 0:
                last_land[...] = held
                continue
            for v in range(blocks):
                base = volume_ref[v] if p == 0 and side == 1 else part_ref[v]
                part_ref[v] = base - step_size * dot(wt_ref[2 * p + 1 - side, v], held)
    for p in range(PHASES):
        for k in range(n - 1):
            out(p, k).wait_send()
            back(p, k).wait_send()


def finish_kernel(part_ref, w_ref, land_ref, residual_ref, updated_hbm, residual_hbm, updated, sems):
    blocks = part_ref.shape[0]
    copies = [pltpu.make_async_copy(residual_ref, residual_hbm, sems.at[blocks])]
    copies[0].start()
    for v in range(blocks):
        updated[v] = jnp.maximum(part_ref[v] - step_size * dot(w_ref[v], land_ref[...]), 0.0)
        copies.append(pltpu.make_async_copy(updated.at[v], updated_hbm.at[v], sems.at[v]))
        copies[-1].start()
    for copy in copies:
        copy.wait()


def fused(tiles, volume, tile_voxel, tile_dest, slot_block, tile_count, counts):
    n = lax.axis_size("dom")
    slots, rows, cols = tiles.shape
    blocks, _, lanes = volume.shape
    buckets = n * blocks
    pairs = round_up((slots + buckets + 1) // 2, UNROLL * REPEAT)
    width = round_up(2 * pairs, 128)
    step = rows // PHASES
    half = n // 2
    vmem = pl.BlockSpec(memory_space=pltpu.VMEM)
    hbm = pl.BlockSpec(memory_space=pltpu.HBM)
    low = jnp.bfloat16
    blocks_of = (PHASES, n, step, lanes)
    handed = pl.pallas_call(
        functools.partial(main_kernel, n),
        out_shape=(
            pltpu.VMEM(volume.shape, jnp.float32),
            pltpu.VMEM((blocks, cols, half * step), low),
            pltpu.VMEM((half * step, lanes), low),
            pltpu.VMEM(counts.shape, low),
        ),
        in_specs=[pl.BlockSpec(memory_space=pltpu.SMEM)] + [hbm] * 6,
        out_specs=(vmem,) * 4,
        scratch_shapes=[pltpu.VMEM((slots + 1, step, cols), low)] * PHASES
        + [pltpu.VMEM((pairs + 1, step, cols), low)] * PHASES
        + [
            pltpu.SMEM(slot_block.shape, jnp.int32),
            pltpu.SMEM((width,), jnp.int32),
            pltpu.SMEM((width,), jnp.int32),
            pltpu.SMEM((width,), jnp.int32),
            pltpu.VMEM((slots,), jnp.int32),
            pltpu.VMEM((slots,), jnp.int32),
            pltpu.VMEM((8, width), jnp.int32),
            pltpu.VMEM(volume.shape, jnp.float32),
            pltpu.VMEM(counts.shape, jnp.int32),
            pltpu.VMEM((blocks * cols, lanes), low),
            pltpu.VMEM(counts.shape, jnp.float32),
        ]
        + [pltpu.VMEM(blocks_of, low)] * 4
        + [
            pltpu.VMEM((2 * PHASES - 1, blocks, cols, half * step), low),
            pltpu.SemaphoreType.DMA((8,)),
            pltpu.SemaphoreType.DMA((PHASES, LOADS)),
        ]
        + [pltpu.SemaphoreType.DMA((PHASES, n))] * 4,
        compiler_params=pltpu.CompilerParams(
            collective_id=0, has_side_effects=True, vmem_limit_bytes=MAIN_VMEM),
        name="exchange",
    )(tile_count, tile_dest, tile_voxel, slot_block, volume, counts, tiles)
    return pl.pallas_call(
        finish_kernel,
        out_shape=(
            jax.ShapeDtypeStruct(volume.shape, jnp.float32),
            jax.ShapeDtypeStruct(counts.shape, low),
        ),
        in_specs=[vmem] * 4,
        out_specs=(hbm, hbm),
        scratch_shapes=[
            pltpu.VMEM(volume.shape, jnp.float32),
            pltpu.SemaphoreType.DMA((blocks + 1,)),
        ],
        compiler_params=pltpu.CompilerParams(vmem_limit_bytes=FINISH_VMEM),
        name="finish",
    )(*handed)


def general(tiles, volume, tile_voxel, tile_dest, slot_block, tile_count, counts):
    n = lax.axis_size("dom")
    slots, rows, cols = tiles.shape
    blocks, _, lanes = volume.shape
    low = jnp.bfloat16
    alive = jnp.arange(slots, dtype=jnp.int32) < tile_count[0]
    bucket = jnp.where(alive, tile_dest * blocks + tile_voxel, -1)
    hot = (bucket[None, :] == jnp.arange(n * blocks, dtype=jnp.int32)[:, None]).astype(low)
    w = jnp.einsum("gt,tab->gab", hot, tiles, preferred_element_type=jnp.float32).astype(low)
    w = w.reshape(n, blocks, rows, cols)
    outgoing = jnp.einsum("dvab,vbs->das", w, volume.astype(low), preferred_element_type=jnp.float32)
    incoming = lax.all_to_all(outgoing.astype(low), "dom", split_axis=0, concat_axis=0, tiled=True)
    owner = (slot_block[0][None, :] == jnp.arange(counts.shape[0], dtype=jnp.int32)[:, None]).astype(low)
    sinogram = jnp.einsum("bd,das->bas", owner, incoming, preferred_element_type=jnp.float32)
    measured = jnp.log(flux / counts.astype(jnp.float32))
    residual = (sinogram - measured).astype(low)
    answers = jnp.einsum("bd,bas->das", owner, residual, preferred_element_type=jnp.float32).astype(low)
    returned = lax.all_to_all(answers, "dom", split_axis=0, concat_axis=0, tiled=True)
    gradient = jnp.einsum("dvab,das->vbs", w, returned, preferred_element_type=jnp.float32)
    return jnp.maximum(volume - step_size * gradient, 0.0), residual


def on_device(tiles, volume, *rest):
    n = lax.axis_size("dom")
    slots, rows, cols = tiles.shape
    need = tiles.size * 2 + n * volume.shape[0] * rows * cols * 6
    if need > VMEM_BUDGET or n & (n - 1) or n < 4 or slots % LOADS or rows != cols or rows % (16 * PHASES):
        return general(tiles, volume, *rest)
    return fused(tiles, volume, *rest)


def solution(mesh):
    both = P(("slab", "dom"), None, None)
    in_specs = (P("dom", None, None), both, P("dom"), P("dom"), P("dom", None), P("dom"), both)
    return jax.shard_map(on_device, mesh=mesh, in_specs=in_specs, out_specs=(both, both), check_vma=False)
```

```python
import functools

import jax
import jax.numpy as jnp
from jax import lax
from jax.experimental import pallas as pl
from jax.experimental.pallas import tpu as pltpu
from jax.sharding import PartitionSpec as P

flux = 32768.0
step_size = 0.5
PHASES = 2
LOADS = 4
GATHER = 2
UNROLL = 8
REPEAT = 2
MAIN_VMEM = 58 * 1024 * 1024
FINISH_VMEM = 10 * 1024 * 1024
VMEM_BUDGET = 18 * 1024 * 1024
MESH = pl.DeviceIdType.MESH


def round_up(x, m):
    return (x + m - 1) // m * m


def peer_masks(n):
    chips = n // 2
    far_first = sorted(range(1, chips), key=lambda k: (k.bit_length() != (chips - 1).bit_length(), k))
    masks = []
    for k in far_first:
        masks += [2 * k, 2 * k + 1]
    return masks + [1, 0]


def dot(a, b, dims=((1,), (0,))):
    return lax.dot_general(a, b, (dims, ((), ())), preferred_element_type=jnp.float32)


def plan_lists(count, dest, voxel, order, blocks, groups, plan_ref, keep_ref):
    slots = dest.shape[1]
    width = plan_ref.shape[1]
    n = len(order)
    buckets = n * blocks
    low = jnp.bfloat16
    rank = jnp.zeros_like(dest)
    for k in range(1, n):
        rank = jnp.where(dest == order[k], k, rank)
    lane = lax.broadcasted_iota(jnp.int32, (1, slots), 1)
    key = jnp.where(lane < count, rank * blocks + voxel, -1)
    b = lax.broadcasted_iota(jnp.int32, (buckets, slots), 0)
    member = key == b
    hot = member.astype(jnp.float32)
    hot_low = hot.astype(low)
    i = lax.broadcasted_iota(jnp.int32, (slots, slots), 0)
    j = lax.broadcasted_iota(jnp.int32, (slots, slots), 1)
    before = dot(hot_low, (i < j).astype(jnp.float32).astype(low))
    held = jnp.floor((jnp.sum(hot, axis=1, keepdims=True) + (GATHER - 1.0)) * (1.0 / GATHER))
    row_count = dot(jnp.ones((8, slots), low), hot_low, ((1,), (1,)))
    row_held = jnp.floor((row_count + (GATHER - 1.0)) * (1.0 / GATHER))
    bi = lax.broadcasted_iota(jnp.int32, (buckets, buckets), 0)
    bj = lax.broadcasted_iota(jnp.int32, (buckets, buckets), 1)
    upper = (bi < bj).astype(jnp.float32).astype(low)
    lower = (bj < bi).astype(jnp.float32).astype(low)
    row_off = dot(row_held.astype(low), upper)
    off = dot(lower, jnp.broadcast_to(held, (buckets, 128)).astype(low))[:, :1]
    place = jnp.sum(jnp.where(member, before + float(GATHER) * off, 0.0), axis=0, keepdims=True)
    place = jnp.where(key < 0, -1, place.astype(jnp.int32))
    p = lax.broadcasted_iota(jnp.int32, (width, slots), 0)
    chosen = (place == p).astype(jnp.float32).astype(low)
    r = lax.broadcasted_iota(jnp.int32, (8, slots), 0)
    t = lax.broadcasted_iota(jnp.int32, (8, slots), 1)
    digits = jnp.where(r == 0, t // 16, jnp.where(r == 1, t % 16, 1)).astype(jnp.float32).astype(low)
    found = dot(digits, chosen, ((1,), (1,)))
    tile = found[0:1] * 16.0 + found[1:2] + (1.0 - found[2:3]) * float(slots)
    plan_ref[0:1, :] = jnp.clip(tile.astype(jnp.int32), 0, slots)
    group = lax.broadcasted_iota(jnp.int32, (groups, buckets), 0)
    first = (row_off[0:1].astype(jnp.int32) == group) & (row_held[0:1] > 0.0)
    starts = jnp.sum(jnp.where(first, 1.0, 0.0), axis=1, keepdims=True)
    keep_ref[...] = jnp.broadcast_to(1.0 - starts, keep_ref.shape)
    last = jnp.where(row_held > 0.0, row_off + row_held - 1.0, float(groups))
    plan_ref[1:2, 0:buckets] = jnp.clip(last[0:1].astype(jnp.int32), 0, groups)


def main_kernel(n, count_ref, dest_hbm, voxel_hbm, slot_hbm, volume_hbm, counts_hbm, tiles_hbm, *refs):
    (part_ref, last_w, last_land, residual_ref), scratch = refs[:4], refs[4:]
    bufs, stores, scratch = scratch[:PHASES], scratch[PHASES:2 * PHASES], scratch[2 * PHASES:]
    (slot_ref, list_s, last_s, dest_ref, voxel_ref, plan_ref, keep_ref, volume_ref, counts_ref, low, measured,
     out_buf, in_buf, answer_buf, landing, wt_ref, small_sems, tile_sems,
     out_send, out_recv, back_send, back_recv) = scratch
    me = lax.axis_index("dom")
    slots = tiles_hbm.shape[0]
    blocks, rows, lanes = volume_ref.shape
    owned = counts_ref.shape[0]
    step = rows // PHASES
    groups = stores[0].shape[0] - 1
    masks = peer_masks(n)
    order = [me ^ m for m in masks]
    half = n // 2
    group = slots // LOADS
    z = me // 2
    swap = ((z + 1) // 2 + 1) % 2 * 2 if half == 4 else 0
    send_order = [[k + swap if k < 2 else k - swap for k in range(half)], list(range(half, n - 1))]

    small = [
        pltpu.make_async_copy(src, dst, small_sems.at[i])
        for i, (src, dst) in enumerate((
            (dest_hbm, dest_ref), (voxel_hbm, voxel_ref), (slot_hbm, slot_ref),
            (volume_hbm, volume_ref), (counts_hbm, counts_ref)))
    ]

    def fetch(p, g):
        at = pl.ds(g * group, group)
        return pltpu.make_async_copy(
            tiles_hbm.at[at, pl.ds(p * step, step)], bufs[p].at[at], tile_sems.at[p, g])

    for copy in small[:3]:
        copy.start()
    for g in range(LOADS):
        fetch(0, g).start()
    barrier = pltpu.get_barrier_semaphore()
    for peer in order[:-1]:
        pl.semaphore_signal(barrier, inc=1, device_id={"dom": peer}, device_id_type=MESH)
    for copy in small[3:5]:
        copy.start()
    for p in range(1, PHASES):
        for g in range(LOADS):
            fetch(p, g).start()

    for copy in small[:3]:
        copy.wait()
    plan_ref[...] = jnp.zeros_like(plan_ref)
    plan_lists(count_ref[0], dest_ref[...].reshape(1, slots), voxel_ref[...].reshape(1, slots), order, blocks, groups, plan_ref, keep_ref)
    to_smem = [
        pltpu.make_async_copy(plan_ref.at[r], dst, small_sems.at[5 + r])
        for r, dst in enumerate((list_s, last_s))
    ]
    for copy in to_smem:
        copy.start()

    for p in range(PHASES):
        bufs[p][slots] = jnp.zeros((step, rows), jnp.bfloat16)
        stores[p][groups] = jnp.zeros((step, rows), jnp.bfloat16)
    for copy in to_smem:
        copy.wait()

    def fold(p):
        buf, store = bufs[p], stores[p]

        def body(i, total):
            first = i * UNROLL
            done = []
            for u in range(UNROLL):
                tiles = [buf[list_s[GATHER * (first + u) + t]] for t in range(GATHER)]
                while len(tiles) > 1:
                    tiles = [a + b for a, b in zip(tiles[::2], tiles[1::2])]
                added = tiles[0].astype(jnp.float32)
                total = total * keep_ref[pl.ds(first + u, 1), :] + added
                done.append(total.astype(jnp.bfloat16))
            for u in range(UNROLL):
                store[first + u] = done[u]
            return total

        lax.fori_loop(0, groups // UNROLL, body, jnp.zeros((step, rows), jnp.float32), unroll=REPEAT)

    def summed(p, k, v):
        return stores[p][last_s[k * blocks + v]]

    def project(p, ks):
        w = jnp.concatenate(
            [jnp.concatenate([summed(p, k, v) for v in range(blocks)], axis=1) for k in ks], axis=0)
        return dot(w, low[...]).astype(jnp.bfloat16)

    def transposed(p, side, v):
        w = jnp.concatenate([summed(p, side * half + k, v) for k in range(half)], axis=0)
        return w.T

    def peer_of(k):
        if isinstance(k, int):
            return order[k]
        return me ^ (half + k)

    def send(src, dst, send_sems, recv_sems, p, k):
        return pltpu.make_async_remote_copy(
            src_ref=src.at[p, k], dst_ref=dst.at[p, k], send_sem=send_sems.at[p, k], recv_sem=recv_sems.at[p, k],
            device_id={"dom": peer_of(k)}, device_id_type=MESH)

    def out(p, k):
        return send(out_buf, in_buf, out_send, out_recv, p, k)

    def back(p, k):
        return send(answer_buf, landing, back_send, back_recv, p, k)

    for p in range(PHASES):
        for g in range(LOADS):
            fetch(p, g).wait()
        fold(p)
        if p == 0:
            small[3].wait()
            for v in range(blocks):
                low[v * rows:(v + 1) * rows, :] = volume_ref[v].astype(jnp.bfloat16)
        for side in range(2):
            ks = range(side * half, side * half + half)
            y = project(p, ks)
            for i, k in enumerate(ks):
                (out_buf if k < n - 1 else in_buf)[p, k] = y[i * step:(i + 1) * step]
            if p == 0 and side == 0:
                pl.semaphore_wait(barrier, n - 1)
            for k in send_order[side]:
                out(p, k).start()

    small[4].wait()
    for b in range(owned):
        measured[b] = jnp.log(flux / counts_ref[b].astype(jnp.float32))
    slot_of = [slot_ref[0, peer] for peer in order]
    for p in range(PHASES):
        for side in range(2):
            for v in range(blocks):
                if p == PHASES - 1 and side == 0:
                    last_w[v] = transposed(p, side, v)
                else:
                    wt_ref[2 * p + 1 - side, v] = transposed(p, side, v)
        for k in reversed(range(n - 1)):
            out(p, k).wait_recv()
        at = slice(p * step, (p + 1) * step)
        for b in range(owned):
            total = jnp.zeros((step, lanes), jnp.float32)
            for k in range(n):
                total += jnp.where(slot_of[k] == b, in_buf[p, k].astype(jnp.float32), 0.0)
            residual_ref[b, at, :] = (total - measured[b, at, :]).astype(jnp.bfloat16)
        for k in range(n - 1):
            answer_buf[p, k] = residual_ref[slot_of[k], at, :]
        for k in send_order[0] + send_order[1]:
            back(p, k).start()
        landing[p, n - 1] = residual_ref[slot_of[n - 1], at, :]

    for p in range(PHASES):
        for side in (1, 0):
            for k in range(side * half, side * half + half):
                if k < n - 1:
                    back(p, k).wait_recv()
            held = landing[p, side * half:(side + 1) * half].reshape(half * step, lanes)
            if p == PHASES - 1 and side == 0:
                last_land[...] = held
                continue
            for v in range(blocks):
                base = volume_ref[v] if p == 0 and side == 1 else part_ref[v]
                part_ref[v] = base - step_size * dot(wt_ref[2 * p + 1 - side, v], held)
    for p in range(PHASES):
        for k in range(n - 1):
            out(p, k).wait_send()
            back(p, k).wait_send()


def finish_kernel(part_ref, w_ref, land_ref, residual_ref, updated_hbm, residual_hbm, updated, sems):
    blocks = part_ref.shape[0]
    copies = [pltpu.make_async_copy(residual_ref, residual_hbm, sems.at[blocks])]
    copies[0].start()
    for v in range(blocks):
        updated[v] = jnp.maximum(part_ref[v] - step_size * dot(w_ref[v], land_ref[...]), 0.0)
        copies.append(pltpu.make_async_copy(updated.at[v], updated_hbm.at[v], sems.at[v]))
        copies[-1].start()
    for copy in copies:
        copy.wait()


def fused(tiles, volume, tile_voxel, tile_dest, slot_block, tile_count, counts):
    n = lax.axis_size("dom")
    slots, rows, cols = tiles.shape
    blocks, _, lanes = volume.shape
    buckets = n * blocks
    groups = round_up((slots + buckets * (GATHER - 1)) // GATHER, UNROLL * REPEAT)
    width = round_up(GATHER * groups, 128)
    step = rows // PHASES
    half = n // 2
    vmem = pl.BlockSpec(memory_space=pltpu.VMEM)
    hbm = pl.BlockSpec(memory_space=pltpu.HBM)
    low = jnp.bfloat16
    blocks_of = (PHASES, n, step, lanes)
    handed = pl.pallas_call(
        functools.partial(main_kernel, n),
        out_shape=(
            pltpu.VMEM(volume.shape, jnp.float32),
            pltpu.VMEM((blocks, cols, half * step), low),
            pltpu.VMEM((half * step, lanes), low),
            pltpu.VMEM(counts.shape, low),
        ),
        in_specs=[pl.BlockSpec(memory_space=pltpu.SMEM)] + [hbm] * 6,
        out_specs=(vmem,) * 4,
        scratch_shapes=[pltpu.VMEM((slots + 1, step, cols), low)] * PHASES
        + [pltpu.VMEM((groups + 1, step, cols), low)] * PHASES
        + [
            pltpu.SMEM(slot_block.shape, jnp.int32),
            pltpu.SMEM((width,), jnp.int32),
            pltpu.SMEM((width,), jnp.int32),
            pltpu.VMEM((slots,), jnp.int32),
            pltpu.VMEM((slots,), jnp.int32),
            pltpu.VMEM((8, width), jnp.int32),
            pltpu.VMEM((groups, 128), jnp.float32),
            pltpu.VMEM(volume.shape, jnp.float32),
            pltpu.VMEM(counts.shape, jnp.int32),
            pltpu.VMEM((blocks * cols, lanes), low),
            pltpu.VMEM(counts.shape, jnp.float32),
        ]
        + [pltpu.VMEM(blocks_of, low)] * 4
        + [
            pltpu.VMEM((2 * PHASES - 1, blocks, cols, half * step), low),
            pltpu.SemaphoreType.DMA((7,)),
            pltpu.SemaphoreType.DMA((PHASES, LOADS)),
        ]
        + [pltpu.SemaphoreType.DMA((PHASES, n))] * 4,
        compiler_params=pltpu.CompilerParams(
            collective_id=0, has_side_effects=True, vmem_limit_bytes=MAIN_VMEM),
        name="exchange",
    )(tile_count, tile_dest, tile_voxel, slot_block, volume, counts, tiles)
    return pl.pallas_call(
        finish_kernel,
        out_shape=(
            jax.ShapeDtypeStruct(volume.shape, jnp.float32),
            jax.ShapeDtypeStruct(counts.shape, low),
        ),
        in_specs=[vmem] * 4,
        out_specs=(hbm, hbm),
        scratch_shapes=[
            pltpu.VMEM(volume.shape, jnp.float32),
            pltpu.SemaphoreType.DMA((blocks + 1,)),
        ],
        compiler_params=pltpu.CompilerParams(vmem_limit_bytes=FINISH_VMEM),
        name="finish",
    )(*handed)


def general(tiles, volume, tile_voxel, tile_dest, slot_block, tile_count, counts):
    n = lax.axis_size("dom")
    slots, rows, cols = tiles.shape
    blocks, _, lanes = volume.shape
    low = jnp.bfloat16
    alive = jnp.arange(slots, dtype=jnp.int32) < tile_count[0]
    bucket = jnp.where(alive, tile_dest * blocks + tile_voxel, -1)
    hot = (bucket[None, :] == jnp.arange(n * blocks, dtype=jnp.int32)[:, None]).astype(low)
    w = jnp.einsum("gt,tab->gab", hot, tiles, preferred_element_type=jnp.float32).astype(low)
    w = w.reshape(n, blocks, rows, cols)
    outgoing = jnp.einsum("dvab,vbs->das", w, volume.astype(low), preferred_element_type=jnp.float32)
    incoming = lax.all_to_all(outgoing.astype(low), "dom", split_axis=0, concat_axis=0, tiled=True)
    owner = (slot_block[0][None, :] == jnp.arange(counts.shape[0], dtype=jnp.int32)[:, None]).astype(low)
    sinogram = jnp.einsum("bd,das->bas", owner, incoming, preferred_element_type=jnp.float32)
    measured = jnp.log(flux / counts.astype(jnp.float32))
    residual = (sinogram - measured).astype(low)
    answers = jnp.einsum("bd,bas->das", owner, residual, preferred_element_type=jnp.float32).astype(low)
    returned = lax.all_to_all(answers, "dom", split_axis=0, concat_axis=0, tiled=True)
    gradient = jnp.einsum("dvab,das->vbs", w, returned, preferred_element_type=jnp.float32)
    return jnp.maximum(volume - step_size * gradient, 0.0), residual


def on_device(tiles, volume, *rest):
    n = lax.axis_size("dom")
    slots, rows, cols = tiles.shape
    need = tiles.size * 2 + n * volume.shape[0] * rows * cols * 6
    if need > VMEM_BUDGET or n & (n - 1) or n < 4 or slots % LOADS or rows != cols or rows % (16 * PHASES):
        return general(tiles, volume, *rest)
    return fused(tiles, volume, *rest)


def solution(mesh):
    both = P(("slab", "dom"), None, None)
    in_specs = (P("dom", None, None), both, P("dom"), P("dom"), P("dom", None), P("dom"), both)
    return jax.shard_map(on_device, mesh=mesh, in_specs=in_specs, out_specs=(both, both), check_vma=False)
```

```python
import functools

import jax
import jax.numpy as jnp
from jax import lax
from jax.experimental import pallas as pl
from jax.experimental.pallas import tpu as pltpu
from jax.sharding import PartitionSpec as P

flux = 32768.0
step_size = 0.5
PHASES = 2
LOADS = 4
GATHER = 2
UNROLL = 8
REPEAT = 2
MAIN_VMEM = 58 * 1024 * 1024
FINISH_VMEM = 10 * 1024 * 1024
VMEM_BUDGET = 18 * 1024 * 1024
MESH = pl.DeviceIdType.MESH


def round_up(x, m):
    return (x + m - 1) // m * m


def peer_masks(n):
    chips = n // 2
    far_first = sorted(range(1, chips), key=lambda k: (k.bit_length() != (chips - 1).bit_length(), k))
    masks = []
    for k in far_first:
        masks += [2 * k, 2 * k + 1]
    return masks + [1, 0]


def dot(a, b, dims=((1,), (0,))):
    return lax.dot_general(a, b, (dims, ((), ())), preferred_element_type=jnp.float32)


def plan_lists(count, dest, voxel, order, blocks, groups, plan_ref, keep_ref):
    slots = dest.shape[1]
    width = plan_ref.shape[1]
    n = len(order)
    buckets = n * blocks
    low = jnp.bfloat16
    rank = jnp.zeros_like(dest)
    for k in range(1, n):
        rank = jnp.where(dest == order[k], k, rank)
    lane = lax.broadcasted_iota(jnp.int32, (1, slots), 1)
    key = jnp.where(lane < count, rank * blocks + voxel, -1)
    b = lax.broadcasted_iota(jnp.int32, (buckets, slots), 0)
    member = key == b
    hot = member.astype(jnp.float32)
    hot_low = hot.astype(low)
    i = lax.broadcasted_iota(jnp.int32, (slots, slots), 0)
    j = lax.broadcasted_iota(jnp.int32, (slots, slots), 1)
    before = dot(hot_low, (i < j).astype(jnp.float32).astype(low))
    held = jnp.floor((jnp.sum(hot, axis=1, keepdims=True) + (GATHER - 1.0)) * (1.0 / GATHER))
    row_count = dot(jnp.ones((8, slots), low), hot_low, ((1,), (1,)))
    row_held = jnp.floor((row_count + (GATHER - 1.0)) * (1.0 / GATHER))
    bi = lax.broadcasted_iota(jnp.int32, (buckets, buckets), 0)
    bj = lax.broadcasted_iota(jnp.int32, (buckets, buckets), 1)
    upper = (bi < bj).astype(jnp.float32).astype(low)
    lower = (bj < bi).astype(jnp.float32).astype(low)
    row_off = dot(row_held.astype(low), upper)
    off = dot(lower, jnp.broadcast_to(held, (buckets, 128)).astype(low))[:, :1]
    place = jnp.sum(jnp.where(member, before + float(GATHER) * off, 0.0), axis=0, keepdims=True)
    place = jnp.where(key < 0, -1, place.astype(jnp.int32))
    p = lax.broadcasted_iota(jnp.int32, (width, slots), 0)
    chosen = (place == p).astype(jnp.float32).astype(low)
    r = lax.broadcasted_iota(jnp.int32, (8, slots), 0)
    t = lax.broadcasted_iota(jnp.int32, (8, slots), 1)
    digits = jnp.where(r == 0, t // 16, jnp.where(r == 1, t % 16, 1)).astype(jnp.float32).astype(low)
    found = dot(digits, chosen, ((1,), (1,)))
    tile = found[0:1] * 16.0 + found[1:2] + (1.0 - found[2:3]) * float(slots)
    plan_ref[0:1, :] = jnp.clip(tile.astype(jnp.int32), 0, slots)
    group = lax.broadcasted_iota(jnp.int32, (groups, buckets), 0)
    first = (row_off[0:1].astype(jnp.int32) == group) & (row_held[0:1] > 0.0)
    starts = jnp.sum(jnp.where(first, 1.0, 0.0), axis=1, keepdims=True)
    keep_ref[...] = jnp.broadcast_to(1.0 - starts, keep_ref.shape)
    last = jnp.where(row_held > 0.0, row_off + row_held - 1.0, float(groups))
    plan_ref[1:2, 0:buckets] = jnp.clip(last[0:1].astype(jnp.int32), 0, groups)


def main_kernel(n, count_ref, dest_hbm, voxel_hbm, slot_hbm, volume_hbm, counts_hbm, tiles_hbm, *refs):
    (part_ref, last_w, last_land, residual_ref), scratch = refs[:4], refs[4:]
    bufs, stores, scratch = scratch[:PHASES], scratch[PHASES:2 * PHASES], scratch[2 * PHASES:]
    (slot_ref, list_s, last_s, dest_ref, voxel_ref, plan_ref, keep_ref, volume_ref, counts_ref, low, measured,
     out_buf, in_buf, answer_buf, landing, wt_ref, small_sems, tile_sems,
     out_send, out_recv, back_send, back_recv) = scratch
    me = lax.axis_index("dom")
    slots = tiles_hbm.shape[0]
    blocks, rows, lanes = volume_ref.shape
    owned = counts_ref.shape[0]
    step = rows // PHASES
    groups = stores[0].shape[0] - 1
    masks = peer_masks(n)
    order = [me ^ m for m in masks]
    half = n // 2
    group = slots // LOADS
    z = me // 2
    swap = ((z + 1) // 2 + 1) % 2 * 2 if half == 4 else 0
    send_order = [[k + swap if k < 2 else k - swap for k in range(half)], list(range(half, n - 1))]

    barrier = pltpu.get_barrier_semaphore()
    for peer in order[:-1]:
        pl.semaphore_signal(barrier, inc=1, device_id={"dom": peer}, device_id_type=MESH)

    small = [
        pltpu.make_async_copy(src, dst, small_sems.at[i])
        for i, (src, dst) in enumerate((
            (dest_hbm, dest_ref), (voxel_hbm, voxel_ref), (slot_hbm, slot_ref),
            (volume_hbm, volume_ref), (counts_hbm, counts_ref)))
    ]

    def fetch(p, g):
        at = pl.ds(g * group, group)
        return pltpu.make_async_copy(
            tiles_hbm.at[at, pl.ds(p * step, step)], bufs[p].at[at], tile_sems.at[p, g])

    for copy in small[:3]:
        copy.start()
    for g in range(LOADS):
        fetch(0, g).start()
    small[3].start()

    for copy in small[:3]:
        copy.wait()
    plan_ref[...] = jnp.zeros_like(plan_ref)
    plan_lists(count_ref[0], dest_ref[...].reshape(1, slots), voxel_ref[...].reshape(1, slots), order, blocks, groups, plan_ref, keep_ref)
    to_smem = [
        pltpu.make_async_copy(plan_ref.at[r], dst, small_sems.at[5 + r])
        for r, dst in enumerate((list_s, last_s))
    ]
    for copy in to_smem:
        copy.start()

    for p in range(PHASES):
        bufs[p][slots] = jnp.zeros((step, rows), jnp.bfloat16)
        stores[p][groups] = jnp.zeros((step, rows), jnp.bfloat16)
    for copy in to_smem:
        copy.wait()

    def fold(p):
        buf, store = bufs[p], stores[p]

        def body(i, total):
            first = i * UNROLL
            done = []
            for u in range(UNROLL):
                tiles = [buf[list_s[GATHER * (first + u) + t]] for t in range(GATHER)]
                while len(tiles) > 1:
                    tiles = [a + b for a, b in zip(tiles[::2], tiles[1::2])]
                added = tiles[0].astype(jnp.float32)
                total = total * keep_ref[pl.ds(first + u, 1), :] + added
                done.append(total.astype(jnp.bfloat16))
            for u in range(UNROLL):
                store[first + u] = done[u]
            return total

        lax.fori_loop(0, groups // UNROLL, body, jnp.zeros((step, rows), jnp.float32), unroll=REPEAT)

    def summed(p, k, v):
        return stores[p][last_s[k * blocks + v]]

    def project(p, ks):
        w = jnp.concatenate(
            [jnp.concatenate([summed(p, k, v) for v in range(blocks)], axis=1) for k in ks], axis=0)
        return dot(w, low[...]).astype(jnp.bfloat16)

    def transposed(p, side, v):
        w = jnp.concatenate([summed(p, side * half + k, v) for k in range(half)], axis=0)
        return w.T

    def peer_of(k):
        if isinstance(k, int):
            return order[k]
        return me ^ (half + k)

    def send(src, dst, send_sems, recv_sems, p, k):
        return pltpu.make_async_remote_copy(
            src_ref=src.at[p, k], dst_ref=dst.at[p, k], send_sem=send_sems.at[p, k], recv_sem=recv_sems.at[p, k],
            device_id={"dom": peer_of(k)}, device_id_type=MESH)

    def out(p, k):
        return send(out_buf, in_buf, out_send, out_recv, p, k)

    def back(p, k):
        return send(answer_buf, landing, back_send, back_recv, p, k)

    for p in range(PHASES):
        for g in range(LOADS):
            fetch(p, g).wait()
        if p == 0:
            for q in range(1, PHASES):
                for g in range(LOADS):
                    fetch(q, g).start()
        if p == 0:
            small[4].start()
        fold(p)
        if p == 0:
            small[3].wait()
            for v in range(blocks):
                low[v * rows:(v + 1) * rows, :] = volume_ref[v].astype(jnp.bfloat16)
        for side in range(2):
            ks = range(side * half, side * half + half)
            y = project(p, ks)
            for i, k in enumerate(ks):
                (out_buf if k < n - 1 else in_buf)[p, k] = y[i * step:(i + 1) * step]
            if p == 0 and side == 0:
                pl.semaphore_wait(barrier, n - 1)
            for k in send_order[side]:
                out(p, k).start()

    small[4].wait()
    for b in range(owned):
        measured[b] = jnp.log(flux / counts_ref[b].astype(jnp.float32))
    slot_of = [slot_ref[0, peer] for peer in order]
    for p in range(PHASES):
        for side in range(2):
            for v in range(blocks):
                if p == PHASES - 1 and side == 0:
                    last_w[v] = transposed(p, side, v)
                else:
                    wt_ref[2 * p + 1 - side, v] = transposed(p, side, v)
        for k in reversed(range(n - 1)):
            out(p, k).wait_recv()
        at = slice(p * step, (p + 1) * step)
        for b in range(owned):
            total = jnp.zeros((step, lanes), jnp.float32)
            for k in range(n):
                total += jnp.where(slot_of[k] == b, in_buf[p, k].astype(jnp.float32), 0.0)
            residual_ref[b, at, :] = (total - measured[b, at, :]).astype(jnp.bfloat16)
        for k in range(n - 1):
            answer_buf[p, k] = residual_ref[slot_of[k], at, :]
        for k in send_order[0] + send_order[1]:
            back(p, k).start()
        landing[p, n - 1] = residual_ref[slot_of[n - 1], at, :]

    for p in range(PHASES):
        for side in (1, 0):
            for k in range(side * half, side * half + half):
                if k < n - 1:
                    back(p, k).wait_recv()
            held = landing[p, side * half:(side + 1) * half].reshape(half * step, lanes)
            if p == PHASES - 1 and side == 0:
                last_land[...] = held
                continue
            for v in range(blocks):
                base = volume_ref[v] if p == 0 and side == 1 else part_ref[v]
                part_ref[v] = base - step_size * dot(wt_ref[2 * p + 1 - side, v], held)
    for p in range(PHASES):
        for k in range(n - 1):
            out(p, k).wait_send()
            back(p, k).wait_send()


def finish_kernel(part_ref, w_ref, land_ref, residual_ref, updated_hbm, residual_hbm, updated, sems):
    blocks = part_ref.shape[0]
    copies = [pltpu.make_async_copy(residual_ref, residual_hbm, sems.at[blocks])]
    copies[0].start()
    for v in range(blocks):
        updated[v] = jnp.maximum(part_ref[v] - step_size * dot(w_ref[v], land_ref[...]), 0.0)
        copies.append(pltpu.make_async_copy(updated.at[v], updated_hbm.at[v], sems.at[v]))
        copies[-1].start()
    for copy in copies:
        copy.wait()


def fused(tiles, volume, tile_voxel, tile_dest, slot_block, tile_count, counts):
    n = lax.axis_size("dom")
    slots, rows, cols = tiles.shape
    blocks, _, lanes = volume.shape
    buckets = n * blocks
    groups = round_up((slots + buckets * (GATHER - 1)) // GATHER, UNROLL * REPEAT)
    width = round_up(GATHER * groups, 128)
    step = rows // PHASES
    half = n // 2
    vmem = pl.BlockSpec(memory_space=pltpu.VMEM)
    hbm = pl.BlockSpec(memory_space=pltpu.HBM)
    low = jnp.bfloat16
    blocks_of = (PHASES, n, step, lanes)
    handed = pl.pallas_call(
        functools.partial(main_kernel, n),
        out_shape=(
            pltpu.VMEM(volume.shape, jnp.float32),
            pltpu.VMEM((blocks, cols, half * step), low),
            pltpu.VMEM((half * step, lanes), low),
            pltpu.VMEM(counts.shape, low),
        ),
        in_specs=[pl.BlockSpec(memory_space=pltpu.SMEM)] + [hbm] * 6,
        out_specs=(vmem,) * 4,
        scratch_shapes=[pltpu.VMEM((slots + 1, step, cols), low)] * PHASES
        + [pltpu.VMEM((groups + 1, step, cols), low)] * PHASES
        + [
            pltpu.SMEM(slot_block.shape, jnp.int32),
            pltpu.SMEM((width,), jnp.int32),
            pltpu.SMEM((width,), jnp.int32),
            pltpu.VMEM((slots,), jnp.int32),
            pltpu.VMEM((slots,), jnp.int32),
            pltpu.VMEM((8, width), jnp.int32),
            pltpu.VMEM((groups, 128), jnp.float32),
            pltpu.VMEM(volume.shape, jnp.float32),
            pltpu.VMEM(counts.shape, jnp.int32),
            pltpu.VMEM((blocks * cols, lanes), low),
            pltpu.VMEM(counts.shape, jnp.float32),
        ]
        + [pltpu.VMEM(blocks_of, low)] * 4
        + [
            pltpu.VMEM((2 * PHASES - 1, blocks, cols, half * step), low),
            pltpu.SemaphoreType.DMA((7,)),
            pltpu.SemaphoreType.DMA((PHASES, LOADS)),
        ]
        + [pltpu.SemaphoreType.DMA((PHASES, n))] * 4,
        compiler_params=pltpu.CompilerParams(
            collective_id=0, has_side_effects=True, vmem_limit_bytes=MAIN_VMEM),
        name="exchange",
    )(tile_count, tile_dest, tile_voxel, slot_block, volume, counts, tiles)
    return pl.pallas_call(
        finish_kernel,
        out_shape=(
            jax.ShapeDtypeStruct(volume.shape, jnp.float32),
            jax.ShapeDtypeStruct(counts.shape, low),
        ),
        in_specs=[vmem] * 4,
        out_specs=(hbm, hbm),
        scratch_shapes=[
            pltpu.VMEM(volume.shape, jnp.float32),
            pltpu.SemaphoreType.DMA((blocks + 1,)),
        ],
        compiler_params=pltpu.CompilerParams(vmem_limit_bytes=FINISH_VMEM),
        name="finish",
    )(*handed)


def general(tiles, volume, tile_voxel, tile_dest, slot_block, tile_count, counts):
    n = lax.axis_size("dom")
    slots, rows, cols = tiles.shape
    blocks, _, lanes = volume.shape
    low = jnp.bfloat16
    alive = jnp.arange(slots, dtype=jnp.int32) < tile_count[0]
    bucket = jnp.where(alive, tile_dest * blocks + tile_voxel, -1)
    hot = (bucket[None, :] == jnp.arange(n * blocks, dtype=jnp.int32)[:, None]).astype(low)
    w = jnp.einsum("gt,tab->gab", hot, tiles, preferred_element_type=jnp.float32).astype(low)
    w = w.reshape(n, blocks, rows, cols)
    outgoing = jnp.einsum("dvab,vbs->das", w, volume.astype(low), preferred_element_type=jnp.float32)
    incoming = lax.all_to_all(outgoing.astype(low), "dom", split_axis=0, concat_axis=0, tiled=True)
    owner = (slot_block[0][None, :] == jnp.arange(counts.shape[0], dtype=jnp.int32)[:, None]).astype(low)
    sinogram = jnp.einsum("bd,das->bas", owner, incoming, preferred_element_type=jnp.float32)
    measured = jnp.log(flux / counts.astype(jnp.float32))
    residual = (sinogram - measured).astype(low)
    answers = jnp.einsum("bd,bas->das", owner, residual, preferred_element_type=jnp.float32).astype(low)
    returned = lax.all_to_all(answers, "dom", split_axis=0, concat_axis=0, tiled=True)
    gradient = jnp.einsum("dvab,das->vbs", w, returned, preferred_element_type=jnp.float32)
    return jnp.maximum(volume - step_size * gradient, 0.0), residual


def on_device(tiles, volume, *rest):
    n = lax.axis_size("dom")
    slots, rows, cols = tiles.shape
    need = tiles.size * 2 + n * volume.shape[0] * rows * cols * 6
    if need > VMEM_BUDGET or n & (n - 1) or n < 4 or slots % LOADS or rows != cols or rows % (16 * PHASES):
        return general(tiles, volume, *rest)
    return fused(tiles, volume, *rest)


def solution(mesh):
    both = P(("slab", "dom"), None, None)
    in_specs = (P("dom", None, None), both, P("dom"), P("dom"), P("dom", None), P("dom"), both)
    return jax.shard_map(on_device, mesh=mesh, in_specs=in_specs, out_specs=(both, both), check_vma=False)
```

```python
import functools

import jax
import jax.numpy as jnp
from jax import lax
from jax.experimental import pallas as pl
from jax.experimental.pallas import tpu as pltpu
from jax.sharding import PartitionSpec as P

flux = 32768.0
step_size = 0.5
PHASES = 2
LOADS = 1
GATHER = 2
UNROLL = 8
REPEAT = 2
MAIN_VMEM = 58 * 1024 * 1024
FINISH_VMEM = 10 * 1024 * 1024
VMEM_BUDGET = 18 * 1024 * 1024
MESH = pl.DeviceIdType.MESH


def round_up(x, m):
    return (x + m - 1) // m * m


def peer_masks(n):
    chips = n // 2
    far_first = sorted(range(1, chips), key=lambda k: (k.bit_length() != (chips - 1).bit_length(), k))
    masks = []
    for k in far_first:
        masks += [2 * k, 2 * k + 1]
    return masks + [1, 0]


def dot(a, b, dims=((1,), (0,))):
    return lax.dot_general(a, b, (dims, ((), ())), preferred_element_type=jnp.float32)


def plan_lists(count, dest, voxel, order, blocks, groups, plan_ref, keep_ref):
    slots = dest.shape[1]
    width = plan_ref.shape[1]
    n = len(order)
    buckets = n * blocks
    low = jnp.bfloat16
    rank = jnp.zeros_like(dest)
    for k in range(1, n):
        rank = jnp.where(dest == order[k], k, rank)
    lane = lax.broadcasted_iota(jnp.int32, (1, slots), 1)
    key = jnp.where(lane < count, rank * blocks + voxel, -1)
    b = lax.broadcasted_iota(jnp.int32, (buckets, slots), 0)
    member = key == b
    hot = member.astype(jnp.float32)
    hot_low = hot.astype(low)
    i = lax.broadcasted_iota(jnp.int32, (slots, slots), 0)
    j = lax.broadcasted_iota(jnp.int32, (slots, slots), 1)
    before = dot(hot_low, (i < j).astype(jnp.float32).astype(low))
    held = jnp.floor((jnp.sum(hot, axis=1, keepdims=True) + (GATHER - 1.0)) * (1.0 / GATHER))
    row_count = dot(jnp.ones((8, slots), low), hot_low, ((1,), (1,)))
    row_held = jnp.floor((row_count + (GATHER - 1.0)) * (1.0 / GATHER))
    bi = lax.broadcasted_iota(jnp.int32, (buckets, buckets), 0)
    bj = lax.broadcasted_iota(jnp.int32, (buckets, buckets), 1)
    upper = (bi < bj).astype(jnp.float32).astype(low)
    lower = (bj < bi).astype(jnp.float32).astype(low)
    row_off = dot(row_held.astype(low), upper)
    off = dot(lower, jnp.broadcast_to(held, (buckets, 128)).astype(low))[:, :1]
    place = jnp.sum(jnp.where(member, before + float(GATHER) * off, 0.0), axis=0, keepdims=True)
    place = jnp.where(key < 0, -1, place.astype(jnp.int32))
    p = lax.broadcasted_iota(jnp.int32, (width, slots), 0)
    chosen = (place == p).astype(jnp.float32).astype(low)
    r = lax.broadcasted_iota(jnp.int32, (8, slots), 0)
    t = lax.broadcasted_iota(jnp.int32, (8, slots), 1)
    digits = jnp.where(r == 0, t // 16, jnp.where(r == 1, t % 16, 1)).astype(jnp.float32).astype(low)
    found = dot(digits, chosen, ((1,), (1,)))
    tile = found[0:1] * 16.0 + found[1:2] + (1.0 - found[2:3]) * float(slots)
    plan_ref[0:1, :] = jnp.clip(tile.astype(jnp.int32), 0, slots)
    group = lax.broadcasted_iota(jnp.int32, (groups, buckets), 0)
    first = (row_off[0:1].astype(jnp.int32) == group) & (row_held[0:1] > 0.0)
    starts = jnp.sum(jnp.where(first, 1.0, 0.0), axis=1, keepdims=True)
    keep_ref[...] = jnp.broadcast_to(1.0 - starts, keep_ref.shape)
    last = jnp.where(row_held > 0.0, row_off + row_held - 1.0, float(groups))
    plan_ref[1:2, 0:buckets] = jnp.clip(last[0:1].astype(jnp.int32), 0, groups)


def main_kernel(n, count_ref, dest_hbm, voxel_hbm, slot_hbm, volume_hbm, counts_hbm, tiles_hbm, *refs):
    (part_ref, last_w, last_land, residual_ref), scratch = refs[:4], refs[4:]
    bufs, stores, scratch = scratch[:PHASES], scratch[PHASES:2 * PHASES], scratch[2 * PHASES:]
    (slot_ref, list_s, last_s, dest_ref, voxel_ref, plan_ref, keep_ref, volume_ref, counts_ref, low, measured,
     out_buf, in_buf, answer_buf, landing, wt_ref, small_sems, tile_sems,
     out_send, out_recv, back_send, back_recv) = scratch
    me = lax.axis_index("dom")
    slots = tiles_hbm.shape[0]
    blocks, rows, lanes = volume_ref.shape
    owned = counts_ref.shape[0]
    step = rows // PHASES
    groups = stores[0].shape[0] - 1
    masks = peer_masks(n)
    order = [me ^ m for m in masks]
    half = n // 2
    group = slots // LOADS
    z = me // 2
    swap = ((z + 1) // 2 + 1) % 2 * 2 if half == 4 else 0
    send_order = [[k + swap if k < 2 else k - swap for k in range(half)], list(range(half, n - 1))]

    barrier = pltpu.get_barrier_semaphore()
    for peer in order[:-1]:
        pl.semaphore_signal(barrier, inc=1, device_id={"dom": peer}, device_id_type=MESH)

    small = [
        pltpu.make_async_copy(src, dst, small_sems.at[i])
        for i, (src, dst) in enumerate((
            (dest_hbm, dest_ref), (voxel_hbm, voxel_ref), (slot_hbm, slot_ref),
            (volume_hbm, volume_ref), (counts_hbm, counts_ref)))
    ]

    def fetch(p, g):
        at = pl.ds(g * group, group)
        return pltpu.make_async_copy(
            tiles_hbm.at[at, pl.ds(p * step, step)], bufs[p].at[at], tile_sems.at[p, g])

    for copy in small[:3]:
        copy.start()
    for g in range(LOADS):
        fetch(0, g).start()
    small[3].start()

    for copy in small[:3]:
        copy.wait()
    plan_ref[...] = jnp.zeros_like(plan_ref)
    plan_lists(count_ref[0], dest_ref[...].reshape(1, slots), voxel_ref[...].reshape(1, slots), order, blocks, groups, plan_ref, keep_ref)
    to_smem = [
        pltpu.make_async_copy(plan_ref.at[r], dst, small_sems.at[5 + r])
        for r, dst in enumerate((list_s, last_s))
    ]
    for copy in to_smem:
        copy.start()

    for p in range(PHASES):
        bufs[p][slots] = jnp.zeros((step, rows), jnp.bfloat16)
        stores[p][groups] = jnp.zeros((step, rows), jnp.bfloat16)
    for copy in to_smem:
        copy.wait()

    def fold(p):
        buf, store = bufs[p], stores[p]

        def body(i, total):
            first = i * UNROLL
            done = []
            for u in range(UNROLL):
                tiles = [buf[list_s[GATHER * (first + u) + t]] for t in range(GATHER)]
                while len(tiles) > 1:
                    tiles = [a + b for a, b in zip(tiles[::2], tiles[1::2])]
                added = tiles[0].astype(jnp.float32)
                total = total * keep_ref[pl.ds(first + u, 1), :] + added
                done.append(total.astype(jnp.bfloat16))
            for u in range(UNROLL):
                store[first + u] = done[u]
            return total

        lax.fori_loop(0, groups // UNROLL, body, jnp.zeros((step, rows), jnp.float32), unroll=REPEAT)

    def summed(p, k, v):
        return stores[p][last_s[k * blocks + v]]

    def project(p, ks):
        w = jnp.concatenate(
            [jnp.concatenate([summed(p, k, v) for v in range(blocks)], axis=1) for k in ks], axis=0)
        return dot(w, low[...]).astype(jnp.bfloat16)

    def transposed(p, side, v):
        w = jnp.concatenate([summed(p, side * half + k, v) for k in range(half)], axis=0)
        return w.T

    def peer_of(k):
        if isinstance(k, int):
            return order[k]
        return me ^ (half + k)

    def send(src, dst, send_sems, recv_sems, p, k):
        return pltpu.make_async_remote_copy(
            src_ref=src.at[p, k], dst_ref=dst.at[p, k], send_sem=send_sems.at[p, k], recv_sem=recv_sems.at[p, k],
            device_id={"dom": peer_of(k)}, device_id_type=MESH)

    def out(p, k):
        return send(out_buf, in_buf, out_send, out_recv, p, k)

    def back(p, k):
        return send(answer_buf, landing, back_send, back_recv, p, k)

    for p in range(PHASES):
        for g in range(LOADS):
            fetch(p, g).wait()
        if p == 0:
            for q in range(1, PHASES):
                for g in range(LOADS):
                    fetch(q, g).start()
        if p == 0:
            small[4].start()
        fold(p)
        if p == 0:
            small[3].wait()
            for v in range(blocks):
                low[v * rows:(v + 1) * rows, :] = volume_ref[v].astype(jnp.bfloat16)
        for side in range(2):
            ks = range(side * half, side * half + half)
            y = project(p, ks)
            for i, k in enumerate(ks):
                (out_buf if k < n - 1 else in_buf)[p, k] = y[i * step:(i + 1) * step]
            if p == 0 and side == 0:
                pl.semaphore_wait(barrier, n - 1)
            for k in send_order[side]:
                out(p, k).start()

    small[4].wait()
    for b in range(owned):
        measured[b] = jnp.log(flux / counts_ref[b].astype(jnp.float32))
    slot_of = [slot_ref[0, peer] for peer in order]
    for p in range(PHASES):
        for side in range(2):
            for v in range(blocks):
                if p == PHASES - 1 and side == 0:
                    last_w[v] = transposed(p, side, v)
                else:
                    wt_ref[2 * p + 1 - side, v] = transposed(p, side, v)
        at = slice(p * step, (p + 1) * step)
        for side in (1, 0):
            ks = range(side * half, side * half + half)
            for k in ks:
                if k < n - 1:
                    out(p, k).wait_recv()
            for b in range(owned):
                total = -measured[b, at, :]
                for k in ks:
                    total += jnp.where(slot_of[k] == b, in_buf[p, k].astype(jnp.float32), 0.0)
                if side:
                    measured[b, at, :] = -total
                else:
                    residual_ref[b, at, :] = total.astype(jnp.bfloat16)
        for side in range(2):
            for k in range(side * half, min(side * half + half, n - 1)):
                answer_buf[p, k] = residual_ref[slot_of[k], at, :]
            for k in send_order[side]:
                back(p, k).start()
        landing[p, n - 1] = residual_ref[slot_of[n - 1], at, :]

    for p in range(PHASES):
        for side in (1, 0):
            for k in range(side * half, side * half + half):
                if k < n - 1:
                    back(p, k).wait_recv()
            held = landing[p, side * half:(side + 1) * half].reshape(half * step, lanes)
            if p == PHASES - 1 and side == 0:
                last_land[...] = held
                continue
            for v in range(blocks):
                base = volume_ref[v] if p == 0 and side == 1 else part_ref[v]
                part_ref[v] = base - step_size * dot(wt_ref[2 * p + 1 - side, v], held)
    for p in range(PHASES):
        for k in range(n - 1):
            out(p, k).wait_send()
            back(p, k).wait_send()


def finish_kernel(part_ref, w_ref, land_ref, residual_ref, updated_hbm, residual_hbm, updated, sems):
    blocks = part_ref.shape[0]
    copies = [pltpu.make_async_copy(residual_ref, residual_hbm, sems.at[blocks])]
    copies[0].start()
    for v in range(blocks):
        updated[v] = jnp.maximum(part_ref[v] - step_size * dot(w_ref[v], land_ref[...]), 0.0)
        copies.append(pltpu.make_async_copy(updated.at[v], updated_hbm.at[v], sems.at[v]))
        copies[-1].start()
    for copy in copies:
        copy.wait()


def fused(tiles, volume, tile_voxel, tile_dest, slot_block, tile_count, counts):
    n = lax.axis_size("dom")
    slots, rows, cols = tiles.shape
    blocks, _, lanes = volume.shape
    buckets = n * blocks
    groups = round_up((slots + buckets * (GATHER - 1)) // GATHER, UNROLL * REPEAT)
    width = round_up(GATHER * groups, 128)
    step = rows // PHASES
    half = n // 2
    vmem = pl.BlockSpec(memory_space=pltpu.VMEM)
    hbm = pl.BlockSpec(memory_space=pltpu.HBM)
    low = jnp.bfloat16
    blocks_of = (PHASES, n, step, lanes)
    handed = pl.pallas_call(
        functools.partial(main_kernel, n),
        out_shape=(
            pltpu.VMEM(volume.shape, jnp.float32),
            pltpu.VMEM((blocks, cols, half * step), low),
            pltpu.VMEM((half * step, lanes), low),
            pltpu.VMEM(counts.shape, low),
        ),
        in_specs=[pl.BlockSpec(memory_space=pltpu.SMEM)] + [hbm] * 6,
        out_specs=(vmem,) * 4,
        scratch_shapes=[pltpu.VMEM((slots + 1, step, cols), low)] * PHASES
        + [pltpu.VMEM((groups + 1, step, cols), low)] * PHASES
        + [
            pltpu.SMEM(slot_block.shape, jnp.int32),
            pltpu.SMEM((width,), jnp.int32),
            pltpu.SMEM((width,), jnp.int32),
            pltpu.VMEM((slots,), jnp.int32),
            pltpu.VMEM((slots,), jnp.int32),
            pltpu.VMEM((8, width), jnp.int32),
            pltpu.VMEM((groups, 128), jnp.float32),
            pltpu.VMEM(volume.shape, jnp.float32),
            pltpu.VMEM(counts.shape, jnp.int32),
            pltpu.VMEM((blocks * cols, lanes), low),
            pltpu.VMEM(counts.shape, jnp.float32),
        ]
        + [pltpu.VMEM(blocks_of, low)] * 4
        + [
            pltpu.VMEM((2 * PHASES - 1, blocks, cols, half * step), low),
            pltpu.SemaphoreType.DMA((7,)),
            pltpu.SemaphoreType.DMA((PHASES, LOADS)),
        ]
        + [pltpu.SemaphoreType.DMA((PHASES, n))] * 4,
        compiler_params=pltpu.CompilerParams(
            collective_id=0, has_side_effects=True, vmem_limit_bytes=MAIN_VMEM),
        name="exchange",
    )(tile_count, tile_dest, tile_voxel, slot_block, volume, counts, tiles)
    return pl.pallas_call(
        finish_kernel,
        out_shape=(
            jax.ShapeDtypeStruct(volume.shape, jnp.float32),
            jax.ShapeDtypeStruct(counts.shape, low),
        ),
        in_specs=[vmem] * 4,
        out_specs=(hbm, hbm),
        scratch_shapes=[
            pltpu.VMEM(volume.shape, jnp.float32),
            pltpu.SemaphoreType.DMA((blocks + 1,)),
        ],
        compiler_params=pltpu.CompilerParams(vmem_limit_bytes=FINISH_VMEM),
        name="finish",
    )(*handed)


def general(tiles, volume, tile_voxel, tile_dest, slot_block, tile_count, counts):
    n = lax.axis_size("dom")
    slots, rows, cols = tiles.shape
    blocks, _, lanes = volume.shape
    low = jnp.bfloat16
    alive = jnp.arange(slots, dtype=jnp.int32) < tile_count[0]
    bucket = jnp.where(alive, tile_dest * blocks + tile_voxel, -1)
    hot = (bucket[None, :] == jnp.arange(n * blocks, dtype=jnp.int32)[:, None]).astype(low)
    w = jnp.einsum("gt,tab->gab", hot, tiles, preferred_element_type=jnp.float32).astype(low)
    w = w.reshape(n, blocks, rows, cols)
    outgoing = jnp.einsum("dvab,vbs->das", w, volume.astype(low), preferred_element_type=jnp.float32)
    incoming = lax.all_to_all(outgoing.astype(low), "dom", split_axis=0, concat_axis=0, tiled=True)
    owner = (slot_block[0][None, :] == jnp.arange(counts.shape[0], dtype=jnp.int32)[:, None]).astype(low)
    sinogram = jnp.einsum("bd,das->bas", owner, incoming, preferred_element_type=jnp.float32)
    measured = jnp.log(flux / counts.astype(jnp.float32))
    residual = (sinogram - measured).astype(low)
    answers = jnp.einsum("bd,bas->das", owner, residual, preferred_element_type=jnp.float32).astype(low)
    returned = lax.all_to_all(answers, "dom", split_axis=0, concat_axis=0, tiled=True)
    gradient = jnp.einsum("dvab,das->vbs", w, returned, preferred_element_type=jnp.float32)
    return jnp.maximum(volume - step_size * gradient, 0.0), residual


def on_device(tiles, volume, *rest):
    n = lax.axis_size("dom")
    slots, rows, cols = tiles.shape
    need = tiles.size * 2 + n * volume.shape[0] * rows * cols * 6
    if need > VMEM_BUDGET or n & (n - 1) or n < 4 or slots % LOADS or rows != cols or rows % (16 * PHASES):
        return general(tiles, volume, *rest)
    return fused(tiles, volume, *rest)


def solution(mesh):
    both = P(("slab", "dom"), None, None)
    in_specs = (P("dom", None, None), both, P("dom"), P("dom"), P("dom", None), P("dom"), both)
    return jax.shard_map(on_device, mesh=mesh, in_specs=in_specs, out_specs=(both, both), check_vma=False)
```
